128 devices in a mesh: sub: 16 (over z, y_hi, core), tile: 8 (over y_lo, x).
Axes of the slice: x: 4, y: 4 (y_hi: 2, y_lo: 2; y = y_hi * 2 + y_lo), z: 4, core: 2. Of those that a mesh axis runs over, the one named last changes fastest.
Arguments:
- load_current: float32 [16, 2, 512, 4096], P('sub', None, 'tile'), may hold values from -6 to 6
- diagonal: float32 [16, 2, 512, 4096], P('sub', None, 'tile')
- start_field: float32 [16, 2, 512, 4096], P('sub', None, 'tile'), may hold values from -4 to 4
- block_inverse: float32 [16, 16, 2, 256, 2, 256], P('sub')
- multipliers: float32 [16, 2, 512, 128], P('sub', None, 'tile'), may hold values from -6 to 6
- active_rows: int32 [16], replicated, may hold values from 128 to 512, as said below
- contact_peer: int32 [16, 8], replicated, may hold values from 0 to 15, as said below
- contact_len: int32 [16, 8], replicated, may hold values from 1 to 256, 512 in all within a row
- port_row: int32 [16, 16], P('sub'), may hold values from 0 to 511
- port_col: int32 [16, 16], P('sub'), may hold values from 0 to 3968
- port_current: float32 [16, 2, 16], P('sub'), may hold values from -16 to 16
Outputs:
- solution: float32 [16, 2, 512, 4096], P('sub', None, 'tile')
- next_multipliers: float32 [16, 2, 512, 128], P('sub', None, 'tile')
The draws below stay inside these ranges and needn't reach their ends.
Inputs may be any that keep to these rules, and one draw needn't show every extreme that they name: `active_rows`: at least one subdomain has all 512 lines active. `contact_peer`: a contact never names its own subdomain.
All inputs are finite; a program needn't handle non-finite values.
Results may differ from the reference program's by a relative error of at most 0.0003.
Values sent between devices are 32-bit elements; how exact they have to be, the bound alone decides.
A program may use at most 128 MiB of HBM per device.

```python
import math
import jax
import jax.numpy as jnp
import numpy as np
from jax import lax

W = 4096
B = 256
IB = 128
NC = 8
NP = 16
PB = 128
SWEEPS = 3
ROWS = 512
SUBS = 16
NB = 16


def draw_active_rows(key, part):
    values = jax.random.randint(key, (SUBS,), ROWS // 4, ROWS + 1)
    chosen = jax.random.randint(jax.random.fold_in(key, 7), (), 0, SUBS)
    return jnp.where(jnp.arange(SUBS) == chosen, ROWS, values).astype(jnp.int32)


def draw_contact_peer(key, part):
    offset = jax.random.randint(key, (SUBS, NC), 1, SUBS)
    return ((jnp.arange(SUBS, dtype=jnp.int32)[:, None] + offset) % SUBS).astype(jnp.int32)


def draw_diagonal(key, part):
    first = jax.random.uniform(jax.random.fold_in(key, 1), (SUBS, 1, ROWS, W), jnp.float32, 4.5, 6.0)
    second = jnp.exp(jax.random.uniform(jax.random.fold_in(key, 2), (SUBS, 1, ROWS, W), jnp.float32, jnp.log(0.3), jnp.log(3.0)))
    return jnp.concatenate([first, second], axis=1)


def draw_block_inverse(key, part):
    shape = (SUBS, NB, 2, B, 2, B)
    comp_out = jnp.arange(2)[None, None, :, None, None, None]
    comp_in = jnp.arange(2)[None, None, None, None, :, None]
    node_out = jnp.arange(B)[None, None, None, :, None, None]
    node_in = jnp.arange(B)[None, None, None, None, None, :]
    unit = ((comp_out == comp_in) & (node_out == node_in)).astype(jnp.float32)
    noise = jax.random.normal(key, shape, jnp.float32)
    scale = 0.15
    return scale * (unit + 0.25 * noise / jnp.sqrt(2.0 * B))


def set_ends(result, stream_key, smallest, top_value):
    dims = result.shape
    index_at = [jax.random.randint(jax.random.fold_in(stream_key, axis), (), 0, dims[axis]) for axis in range(len(dims))]
    result = result.at[tuple(index_at)].set(smallest)
    longest = dims.index(max(dims))
    index_at[longest] = (index_at[longest] + 1) % dims[longest]
    return result.at[tuple(index_at)].set(top_value)


def block_scale(own_key, dims, split, smallest, high):
    def one(dim, blocks):
        heights = jax.random.uniform(jax.random.fold_in(jax.random.fold_in(own_key, 6), dim), (blocks,), jnp.float32, smallest / len(split), high / len(split))
        return jnp.repeat(jnp.exp(heights), dims[dim] // blocks).reshape((-1,) + (1,) * (len(dims) - dim - 1))

    factor_of = one(*split[0])
    for cut in split[1:]:
        factor_of = factor_of * one(*cut)
    return factor_of


def split_up(amount, total, reach, skew):
    loads = [(1 << 20) // math.isqrt(standing ** skew) + 1 for standing in range(2, amount + 1)]
    surplus, given = total - reach - (amount - 1), [1] * (amount - 1)
    while surplus > 0:
        candidates = [i for i in range(amount - 1) if given[i] < reach]
        whole, budget = sum([loads[i] for i in candidates]), surplus
        for i in candidates:
            more = min(reach - given[i], max(1, budget * loads[i] // whole), surplus)
            given[i] = given[i] + more
            surplus = surplus - more
    return np.array([reach] + given)


def ragged(stream_key, count, total, bound, skew):
    if count == 2:
        one = jax.random.randint(stream_key, (), max(1, total - bound), min(bound, total - 1) + 1)
        return jnp.stack([one, total - one])
    lengths = jnp.asarray(split_up(count, total, bound, skew), jnp.int32)
    twos = (count - 1) // 2
    donor, sink = lengths[1:1 + 2 * twos:2], lengths[2:2 + 2 * twos:2]
    room = jnp.minimum(donor - 1, bound - sink)
    passed = jax.random.randint(jax.random.fold_in(stream_key, 1), (twos,), 0, 1 << 20) % (room + 1)
    lengths = lengths.at[1:1 + 2 * twos:2].set(donor - passed).at[2:2 + 2 * twos:2].set(sink + passed)
    return lengths[jax.random.permutation(jax.random.fold_in(stream_key, 2), count)]


def bell_draw(rng, shape, deviation, reach, split=(), held_as=jnp.bfloat16):
    gain = block_scale(rng, shape, split, -0.22, 0.18) if split else 1.0
    array = jax.random.normal(rng, shape, jnp.float32) * deviation * gain
    return jnp.minimum(jnp.maximum(array, -reach), reach).astype(held_as)


def setup_inputs(seed: int = 0) -> dict:
    splits = jax.random.split(jax.random.key(seed), 12)
    return {
        "load_current": bell_draw(splits[0], (SUBS, 2, ROWS, W), 1.0, 6.0, ((0, 16), (2, 8)), jnp.float32),
        "diagonal": draw_diagonal(jax.random.fold_in(splits[11], 71), 0),
        "start_field": bell_draw(splits[2], (SUBS, 2, ROWS, W), 0.3, 4.0, ((0, 16), (2, 8)), jnp.float32),
        "block_inverse": draw_block_inverse(jax.random.fold_in(splits[11], 71), 0),
        "multipliers": bell_draw(splits[4], (SUBS, 2, ROWS, IB), 0.5, 6.0, ((0, 16), (2, 8)), jnp.float32),
        "active_rows": draw_active_rows(jax.random.fold_in(splits[11], 71), 0),
        "contact_peer": draw_contact_peer(jax.random.fold_in(splits[11], 71), 0),
        "contact_len": jax.vmap(lambda own: ragged(own, NC, ROWS, ROWS // 2, 2))(jax.random.split(splits[7], SUBS)).reshape((SUBS, NC)).astype(jnp.int32),
        "port_row": set_ends(jax.random.randint(splits[8], (SUBS, NP), 0, ROWS), jax.random.fold_in(splits[8], 1), 0, ROWS - 1).astype(jnp.int32),
        "port_col": set_ends(jax.random.randint(splits[9], (SUBS, NP), 0, W - PB + 1), jax.random.fold_in(splits[9], 1), 0, W - PB).astype(jnp.int32),
        "port_current": bell_draw(splits[10], (SUBS, 2, NP), 3.0, 16.0, ((0, 16),), jnp.float32),
    }


def contract(form, left, right):
    return jnp.einsum(form, left, right, precision=lax.Precision.HIGHEST)


def row_peers(contact_peer, contact_len, first_row, count):
    ends = jnp.cumsum(contact_len, axis=1).astype(jnp.int32)
    starts = ends - contact_len
    lines = first_row + jnp.arange(count, dtype=jnp.int32)
    inside = (lines[None, None, :] >= starts[:, :, None]) & (lines[None, None, :] < ends[:, :, None])
    return jnp.sum(jnp.where(inside, contact_peer[:, :, None], 0), axis=1).astype(jnp.int32)


def ports_source(load, prow, pcol, pcur, lines):
    width = load.shape[2]
    rows_hot = (prow[:, None] == lines[None, :]).astype(jnp.float32)
    columns = jnp.arange(width, dtype=jnp.int32)
    cols_hot = ((columns[None, :] >= pcol[:, None]) & (columns[None, :] < pcol[:, None] + PB)).astype(jnp.float32)
    weighted = pcur[:, :, None] * rows_hot[None]
    return load + contract('cpg,pj->cgj', weighted, cols_hot)


def operate_rows(extended, diag):
    middle = extended[:, 1:-1]
    sides = jnp.pad(middle, ((0, 0), (0, 0), (1, 1)))
    beside = extended[:, :-2] + extended[:, 2:] + sides[:, :, :-2] + sides[:, :, 2:]
    real = diag[0] * middle[0] - diag[1] * middle[1]
    imag = diag[0] * middle[1] + diag[1] * middle[0]
    return jnp.stack([real, imag]) - beside


def relax_lines(extended, source, diag, blocks, mask):
    middle = extended[:, 1:-1]
    resid = source - operate_rows(extended, diag)
    count, width = resid.shape[1], resid.shape[2]
    nblock, bsize = blocks.shape[0], blocks.shape[2]
    update = contract('ncidj,drnj->crni', blocks, resid.reshape(2, count, nblock, bsize)).reshape(2, count, width)
    return mask[None, :, None] * (middle + update)


def reference(load_current, diagonal, start_field, block_inverse, multipliers, active_rows, contact_peer, contact_len, port_row, port_col, port_current):
    peers = row_peers(contact_peer, contact_len, 0, ROWS)
    owners = jnp.arange(SUBS, dtype=jnp.int32)
    hot = (peers[:, None, :] == owners[None, :, None]).astype(jnp.float32)
    incoming = contract('sng,scgj->ncgj', hot, multipliers)
    lines = jnp.arange(ROWS, dtype=jnp.int32)

    def one_domain(items):
        load, diag, start, blocks, mult, inflow, active, prow, pcol, pcur = items
        source = ports_source(load, prow, pcol, pcur, lines)
        source = source.at[:, :, :IB].add(-mult)
        source = source.at[:, :, W - IB:].add(inflow)
        mask = ((lines >= 0) & (lines < active)).astype(jnp.float32)
        field = mask[None, :, None] * start
        for sweep in range(SWEEPS):
            extended = jnp.pad(field, ((0, 0), (1, 1), (0, 0)))
            field = relax_lines(extended, source, diag, blocks, mask)
        return field

    fields = lax.map(one_domain, (load_current, diagonal, start_field, block_inverse, multipliers, incoming, active_rows, port_row, port_col, port_current))
    far = fields[:, :, :, W - IB:]
    peer_end = contract('sng,ncgj->scgj', hot, far)
    return fields, multipliers + (fields[:, :, :, :IB] - peer_end)
```

```python
import functools

import jax
import jax.numpy as jnp
from jax import lax
from jax.experimental import pallas as pl
from jax.experimental.pallas import tpu as pltpu
from jax.sharding import PartitionSpec as P

MESH = pl.DeviceIdType.MESH
BF = jnp.bfloat16
F32 = jnp.float32
NB = 16
ROWS = 64
EARLY = 5
AHEAD = 4

RUNS = (
    (0, 0, 1, 15),
    (1, 0, 1, 11),
    (0, 15, 1, 1),
    (1, 11, 1, 2),
    (2, 0, 1, 4),
    (1, 15, -1, 3),
    (2, 4, 1, 4),
    (2, 15, 1, 1),
    (2, 8, 1, 7),
)
ORDER = [(s, k0 + d * i) for s, k0, d, n in RUNS for i in range(n)]
TOTAL = len(ORDER)
AT = {entry: e for e, entry in enumerate(ORDER)}
AT_INFLOW = AT[(0, 15)]
AT_FAR = AT[(2, 15)]


def check_order():
    assert sorted(ORDER) == [(s, k) for s in range(3) for k in range(NB)]
    for s, k in ORDER:
        if s:
            for j in (k - 1, k, k + 1):
                if 0 <= j < NB:
                    assert AT[(s - 1, j)] + 2 <= AT[(s, k)]


def entry_of(e):
    sweep = jnp.int32(RUNS[0][0])
    block = RUNS[0][1] + RUNS[0][2] * e
    start = RUNS[0][3]
    for s, k0, d, n in RUNS[1:]:
        later = e >= start
        sweep = jnp.where(later, s, sweep)
        block = jnp.where(later, k0 + d * (e - start), block)
        start += n
    return sweep, block


def body(
    load_hbm, diag_hbm, start_hbm, edge_hbm, block_hbm, mult_hbm, active_ref,
    len_hbm, peer_hbm, prow_hbm, pcol_hbm, pcur_hbm,
    out_hbm, next_hbm,
    field, src, diag, stage, upper, lower, lhs,
    held, far, inflow, part, part_in, end_in, ahead_out,
    peers, lens, cpeer, prow, pcol, pcur, weights,
    in_sem, b_sem, small_sem, hs_sem, hr_sem, s1_sem, r1_sem, s2_sem, r2_sem, p_sem, o_sem, n_sem,
):
    sub = lax.axis_index("sub")
    tile = lax.axis_index("tile")
    last_tile = lax.axis_size("tile") - 1
    core = lax.rem(sub, 2)
    place = sub // 2
    places = lax.axis_size("sub") // 2
    partner = place * 2 + (1 - core)
    first_row = tile * ROWS
    has_up = tile > 0
    has_down = tile < last_tile

    def inputs_of(j):
        t = 2 * j
        copies = []
        for c in range(2):
            for h in range(2):
                copies.append(
                    pltpu.make_async_copy(
                        start_hbm.at[0, c, :, pl.ds(pl.multiple_of((t + h) * 128, 128), 128)],
                        field.at[0, c, t + h + 1, pl.ds(8, ROWS), :],
                        in_sem.at[j, 2 * c + h],
                    )
                )
        copies.append(
            pltpu.make_async_copy(
                load_hbm.at[:, :, pl.ds(t, 2)], src.at[:, :, pl.ds(t, 2)], in_sem.at[j, 4]
            )
        )
        copies.append(
            pltpu.make_async_copy(
                diag_hbm.at[:, :, pl.ds(t, 2)], diag.at[:, :, pl.ds(t, 2)], in_sem.at[j, 5]
            )
        )
        return copies

    def blocks_of(j):
        return pltpu.make_async_copy(block_hbm.at[j], stage.at[j], b_sem.at[j])

    def issue(j):
        for copy in inputs_of(j):
            copy.start()
        blocks_of(j).start()

    small = [
        pltpu.make_async_copy(a, b, small_sem.at[i])
        for i, (a, b) in enumerate(
            (
                (len_hbm, lens), (peer_hbm, cpeer), (prow_hbm, prow),
                (pcol_hbm, pcol), (pcur_hbm, pcur),
            )
        )
    ]
    own_mult = pltpu.make_async_copy(mult_hbm.at[0], held.at[place], small_sem.at[5])

    def edge_copy(side, s, k):
        t = 2 * k + 1
        row, there, to = ((8, ROWS + 8, tile - 1), (ROWS + 7, 7, tile + 1))[side]
        return pltpu.make_async_remote_copy(
            src_ref=field.at[s, :, pl.ds(t, 2), pl.ds(row, 1), :],
            dst_ref=field.at[s, :, pl.ds(t, 2), pl.ds(there, 1), :],
            send_sem=hs_sem.at[side, s, k],
            recv_sem=hr_sem.at[side, s, k],
            device_id=(sub, to),
            device_id_type=MESH,
        )

    def first_edge(side):
        group, line, there, to = ((0, 0, ROWS + 8, tile - 1), (7, 7, 7, tile + 1))[side]
        return pltpu.make_async_remote_copy(
            src_ref=edge_hbm.at[:, group, :, pl.ds(line, 1), :],
            dst_ref=field.at[0, :, pl.ds(1, 2 * NB), pl.ds(there, 1), :],
            send_sem=hs_sem.at[side, 0, 0],
            recv_sem=hr_sem.at[side, 0, 0],
            device_id=(sub, to),
            device_id_type=MESH,
        )

    def spread(source, target, send, recv, offset, slot):
        to = lax.rem(place + offset, places)
        return pltpu.make_async_remote_copy(
            src_ref=source,
            dst_ref=target.at[slot],
            send_sem=send.at[offset - 1],
            recv_sem=recv.at[slot],
            device_id=(to * 2 + core, tile),
            device_id_type=MESH,
        )

    def to_partner(source, target, which):
        return pltpu.make_async_remote_copy(
            src_ref=source,
            dst_ref=target,
            send_sem=p_sem.at[2 * which],
            recv_sem=p_sem.at[2 * which + 1],
            device_id=(partner, tile),
            device_id_type=MESH,
        )

    def far_source():
        return field.at[3, :, 2 * NB, pl.ds(8, ROWS), :]

    for copy in small:
        copy.start()
    for j in range(2):
        issue(j)
    own_mult.start()
    barrier = pltpu.get_barrier_semaphore()
    for offset in range(1, 8):
        to = lax.rem(place + offset, places)
        pl.semaphore_signal(barrier, inc=1, device_id=(to * 2 + core, tile), device_id_type=MESH)
    pl.semaphore_signal(barrier, inc=1, device_id=(partner, tile), device_id_type=MESH)

    @pl.when(has_up)
    def _():
        pl.semaphore_signal(barrier, inc=1, device_id=(sub, tile - 1), device_id_type=MESH)

    @pl.when(has_down)
    def _():
        pl.semaphore_signal(barrier, inc=1, device_id=(sub, tile + 1), device_id_type=MESH)

    for j in range(2, EARLY + AHEAD):
        issue(j)

    for s in range(3):
        for c in range(2):
            for t in (0, 2 * NB + 1):
                field[s, c, t, 8 : ROWS + 8, :] = jnp.zeros((ROWS, 128), F32)

    @pl.when(tile == 0)
    def _():
        for s in range(3):
            field[s, :, :, 7:8, :] = jnp.zeros((2, 2 * NB + 2, 1, 128), F32)

    @pl.when(tile == last_tile)
    def _():
        for s in range(3):
            field[s, :, :, ROWS + 8 : ROWS + 9, :] = jnp.zeros((2, 2 * NB + 2, 1, 128), F32)

    for copy in small:
        copy.wait()
    active = active_ref[sub]
    length = lens[...]
    ends = length
    depth = lax.broadcasted_iota(jnp.int32, length.shape, 0)
    for step in (1, 2, 4):
        ends = ends + jnp.where(depth >= step, pltpu.roll(ends, step, 0), 0)
    starts = ends - length
    named = cpeer[...]
    line16 = lax.broadcasted_iota(jnp.int32, (ROWS, 16), 0) + first_row
    found = jnp.zeros((ROWS, 16), jnp.int32)
    for c in range(8):
        inside = (line16 >= starts[c : c + 1, :]) & (line16 < ends[c : c + 1, :])
        found = found + jnp.where(inside, named[c : c + 1, :], 0)
    peers[...] = found.astype(F32)
    rows_hot = (prow[...] == line16).astype(F32)
    for c in range(2):
        weighted = rows_hot * pcur[c : c + 1, :]
        top = weighted.astype(BF)
        weights[c * ROWS : (c + 1) * ROWS, :] = top
        weights[(2 + c) * ROWS : (3 + c) * ROWS, :] = (weighted - top.astype(F32)).astype(BF)
    eye = lax.broadcasted_iota(jnp.int32, (16, 16), 0) == lax.broadcasted_iota(jnp.int32, (16, 16), 1)
    col = jnp.sum(jnp.where(eye, pcol[...].astype(F32), 0.0), axis=1, keepdims=True)

    def line_mask():
        line = lax.broadcasted_iota(jnp.int32, (ROWS, 128), 0) + first_row
        return (line < active).astype(F32)

    def split(j):
        for q in range(4):
            v = stage[j, pl.ds(q, 512, stride=4), :].T
            top = v.astype(BF)
            upper[j, q * 128 : (q + 1) * 128, :] = top
            lower[j, q * 128 : (q + 1) * 128, :] = (v - top.astype(F32)).astype(BF)

    def await_inputs(j):
        for copy in inputs_of(j):
            copy.wait()
        blocks_of(j).wait()

    def prepare(j):
        mask = line_mask()
        at = lax.broadcasted_iota(jnp.int32, (16, 256), 1).astype(F32) + (j * 256).astype(F32)
        cols_hot = ((at >= col) & (at < col + 128.0)).astype(F32).astype(BF)
        fed = jnp.dot(weights[...], cols_hot, preferred_element_type=F32)
        for c in range(2):
            for h in range(2):
                t = 2 * j + h
                field[0, c, t + 1, 8 : ROWS + 8, :] = field[0, c, t + 1, 8 : ROWS + 8, :] * mask
                add = (
                    fed[c * ROWS : (c + 1) * ROWS, h * 128 : (h + 1) * 128]
                    + fed[(2 + c) * ROWS : (3 + c) * ROWS, h * 128 : (h + 1) * 128]
                )
                src[c, :, t] = src[c, :, t] + add.reshape(8, 8, 128)

    def residual(s, k, slot):
        lane = lax.broadcasted_iota(jnp.int32, (ROWS, 128), 1)
        t = 2 * k + 1
        mid, beside = [], []
        for c in range(2):
            tiles = [field[s, c, t + o, 8 : ROWS + 8, :] for o in (-1, 0, 1, 2)]
            right = [pltpu.roll(tiles[i], 1, 1) for i in (0, 1, 2)]
            left = [pltpu.roll(tiles[i], 127, 1) for i in (1, 2, 3)]
            for h in range(2):
                total = (
                    field[s, c, t + h, 7 : ROWS + 7, :]
                    + field[s, c, t + h, 9 : ROWS + 9, :]
                    + jnp.where(lane == 0, right[h], right[h + 1])
                    + jnp.where(lane == 127, left[h + 1], left[h])
                )
                mid.append(tiles[1 + h])
                beside.append(total)
        for h in range(2):
            d0 = diag[0, :, 2 * k + h].reshape(ROWS, 128)
            d1 = diag[1, :, 2 * k + h].reshape(ROWS, 128)
            f0, f1 = mid[h], mid[2 + h]
            s0 = src[0, :, 2 * k + h].reshape(ROWS, 128)
            s1 = src[1, :, 2 * k + h].reshape(ROWS, 128)
            r0 = s0 - (d0 * f0 - d1 * f1 - beside[h])
            r1 = s1 - (d0 * f1 + d1 * f0 - beside[2 + h])
            for d, r in enumerate((r0, r1)):
                q = 2 * h + d
                top = r.astype(BF)
                lhs[slot, 0:ROWS, q * 128 : (q + 1) * 128] = top
                lhs[slot, ROWS : 2 * ROWS, q * 128 : (q + 1) * 128] = (r - top.astype(F32)).astype(BF)

    def relax(s, k, slot):
        both = lhs[slot]
        p = jnp.dot(both, upper[k], preferred_element_type=F32)
        q = jnp.dot(both[:ROWS], lower[k], preferred_element_type=F32)
        z = p[:ROWS] + p[ROWS:] + q
        mask = line_mask()
        for c in range(2):
            for h in range(2):
                t = 2 * k + 1 + h
                a = c * 256 + h * 128
                field[s + 1, c, t, 8 : ROWS + 8, :] = mask * (
                    field[s, c, t, 8 : ROWS + 8, :] + z[:, a : a + 128]
                )

    def send_edges(s, k):
        @pl.when((s < 3) & has_up)
        def _():
            edge_copy(0, s, k).start()

        @pl.when((s < 3) & has_down)
        def _():
            edge_copy(1, s, k).start()

    def await_edges(s, k):
        @pl.when((s > 0) & has_down)
        def _():
            edge_copy(0, s, k).wait_recv()

        @pl.when((s > 0) & has_up)
        def _():
            edge_copy(1, s, k).wait_recv()

    def out_copy(k, c, h):
        t = 2 * k + h
        return pltpu.make_async_copy(
            field.at[3, c, t + 1, pl.ds(8, ROWS), :],
            out_hbm.at[0, c, :, pl.ds(pl.multiple_of(t * 128, 128), 128)],
            o_sem.at[k, 2 * c + h],
        )

    def store_out(s, k):
        @pl.when(s == 2)
        def _():
            for c in range(2):
                for h in range(2):
                    out_copy(k, c, h).start()

    def column(which):
        lane = lax.broadcasted_iota(jnp.int32, (ROWS, 16), 1)
        return jnp.sum(jnp.where(lane == which, peers[...], 0.0), axis=1, keepdims=True)

    await_inputs(0)
    split(0)

    pl.semaphore_wait(barrier, 8 + has_up.astype(jnp.int32) + has_down.astype(jnp.int32))

    @pl.when(has_up)
    def _():
        first_edge(0).start()

    @pl.when(has_down)
    def _():
        first_edge(1).start()

    for offset in range(1, 8):
        spread(mult_hbm.at[0], held, s1_sem, r1_sem, offset, place).start()

    @pl.loop(1, EARLY)
    def _(j):
        await_inputs(j)
        split(j)

    @pl.loop(0, EARLY)
    def _(j):
        prepare(j)

    own_mult.wait()
    for c in range(2):
        src[c, :, 0] = src[c, :, 0] - held[place, c].reshape(8, 8, 128)

    @pl.when(has_down)
    def _():
        first_edge(0).wait_recv()
        scale = jnp.where(first_row + ROWS < active, 1.0, 0.0)
        for c in range(2):
            field[0, c, 1 : 2 * NB + 1, ROWS + 8 : ROWS + 9, :] = (
                field[0, c, 1 : 2 * NB + 1, ROWS + 8 : ROWS + 9, :] * scale
            )

    @pl.when(has_up)
    def _():
        first_edge(1).wait_recv()
        scale = jnp.where(first_row - 1 < active, 1.0, 0.0)
        for c in range(2):
            field[0, c, 1 : 2 * NB + 1, 7:8, :] = field[0, c, 1 : 2 * NB + 1, 7:8, :] * scale

    residual(0, 0, 0)

    @pl.loop(0, NB - EARLY)
    def _(e):
        @pl.when(e + EARLY + AHEAD < NB)
        def _():
            issue(e + EARLY + AHEAD)

        await_inputs(e + EARLY)
        slot = lax.rem(e, 2)
        split(e + EARLY)
        residual(0, e + 1, 1 - slot)
        relax(0, e, slot)
        prepare(e + EARLY)
        send_edges(1, e)

    @pl.loop(NB - EARLY, TOTAL - 1)
    def _(e):
        s, k = entry_of(e)
        s2, k2 = entry_of(e + 1)

        @pl.when(e + 1 == AT_INFLOW - 3)
        def _():
            for offset in range(1, 8):
                j = lax.rem(place + offset, places)
                spread(mult_hbm.at[0], held, s1_sem, r1_sem, offset, j).wait_recv()
            inflow[...] = jnp.zeros_like(inflow)
            part[...] = jnp.zeros_like(part)

            @pl.loop(0, 8)
            def _(j):
                seen = column(2 * j + core)
                mine = seen == sub.astype(F32)
                theirs = seen == partner.astype(F32)
                for c in range(2):
                    v = held[j, c]
                    inflow[c] = inflow[c] + jnp.where(mine, v, 0.0)
                    part[0, c] = part[0, c] + jnp.where(theirs, v, 0.0)

            to_partner(part.at[0], part_in, 0).start()

        @pl.when(e + 1 == AT_INFLOW)
        def _():
            to_partner(part.at[0], part_in, 0).wait_recv()
            for c in range(2):
                total = inflow[c] + part_in[c]
                src[c, :, 2 * NB - 1] = src[c, :, 2 * NB - 1] + total.reshape(8, 8, 128)

        await_edges(s2, k2)
        slot = lax.rem(e, 2)
        residual(s2, k2, 1 - slot)
        relax(s, k, slot)
        send_edges(s + 1, k)
        store_out(s, k)

        @pl.when(e == AT_FAR)
        def _():
            for offset in range(1, 8):
                spread(far_source(), far, s2_sem, r2_sem, offset, place).start()

    s, k = ORDER[-1]
    relax(s, k, (TOTAL - 1) % 2)
    for c in range(2):
        for h in range(2):
            out_copy(k, c, h).start()

    own_peer = column(sub)
    their_peer = column(partner)
    far[place] = field[3, :, 2 * NB, 8 : ROWS + 8, :]
    for offset in range(1, 8):
        j = lax.rem(place + offset, places)
        spread(far_source(), far, s2_sem, r2_sem, offset, j).wait_recv()
    for c in range(2):
        mine = jnp.zeros((ROWS, 128), F32)
        theirs = jnp.zeros((ROWS, 128), F32)
        for j in range(8):
            v = far[j, c]
            at = (2 * j + core).astype(F32)
            mine = mine + jnp.where(own_peer == at, v, 0.0)
            theirs = theirs + jnp.where(their_peer == at, v, 0.0)
        inflow[c] = mine
        part[1, c] = theirs
    to_partner(part.at[1], end_in, 1).start()
    to_partner(part.at[1], end_in, 1).wait_recv()
    for c in range(2):
        ahead_out[c] = held[place, c] + (field[3, c, 1, 8 : ROWS + 8, :] - (inflow[c] + end_in[c]))
    last = pltpu.make_async_copy(ahead_out, next_hbm.at[0], n_sem)
    last.start()

    @pl.when(has_up)
    def _():
        first_edge(0).wait_send()

    @pl.when(has_down)
    def _():
        first_edge(1).wait_send()

    for offset in range(1, 8):
        spread(mult_hbm.at[0], held, s1_sem, r1_sem, offset, place).wait_send()
        spread(far_source(), far, s2_sem, r2_sem, offset, place).wait_send()
    to_partner(part.at[0], part_in, 0).wait_send()
    to_partner(part.at[1], end_in, 1).wait_send()

    @pl.loop(0, NB)
    def _(k):
        for s in (1, 2):
            @pl.when(has_up)
            def _():
                edge_copy(0, s, k).wait_send()

            @pl.when(has_down)
            def _():
                edge_copy(1, s, k).wait_send()

        for c in range(2):
            for h in range(2):
                out_copy(k, c, h).wait()

    last.wait()


def per_device(
    load_current, diagonal, start_field, block_inverse, multipliers, active_rows,
    contact_peer, contact_len, port_row, port_col, port_current,
):
    width = load_current.shape[3]

    def tiled(x):
        return x.reshape(2, 8, 8, width // 128, 128).transpose(0, 1, 3, 2, 4)

    blocks = (
        block_inverse.reshape(NB, 2, 256, 2, 2, 128).transpose(0, 1, 2, 4, 3, 5).reshape(NB, 2048, 128)
    )
    hbm = pl.BlockSpec(memory_space=pl.ANY)
    dma = pltpu.SemaphoreType.DMA
    return pl.pallas_call(
        body,
        out_shape=(
            jax.ShapeDtypeStruct(load_current.shape, F32),
            jax.ShapeDtypeStruct(multipliers.shape, F32),
        ),
        in_specs=[hbm] * 6 + [pl.BlockSpec(memory_space=pltpu.SMEM)] + [hbm] * 5,
        out_specs=(hbm, hbm),
        scratch_shapes=[
            pltpu.VMEM((4, 2, 2 * NB + 2, ROWS + 16, 128), F32),
            pltpu.VMEM((2, 8, 2 * NB, 8, 128), F32),
            pltpu.VMEM((2, 8, 2 * NB, 8, 128), F32),
            pltpu.VMEM((NB, 2048, 128), F32),
            pltpu.VMEM((NB, 512, 512), BF),
            pltpu.VMEM((NB, 512, 512), BF),
            pltpu.VMEM((2, 2 * ROWS, 512), BF),
            pltpu.VMEM((8, 2, ROWS, 128), F32),
            pltpu.VMEM((8, 2, ROWS, 128), F32),
            pltpu.VMEM((2, ROWS, 128), F32),
            pltpu.VMEM((2, 2, ROWS, 128), F32),
            pltpu.VMEM((2, ROWS, 128), F32),
            pltpu.VMEM((2, ROWS, 128), F32),
            pltpu.VMEM((2, ROWS, 128), F32),
            pltpu.VMEM((ROWS, 16), F32),
            pltpu.VMEM((8, 16), jnp.int32),
            pltpu.VMEM((8, 16), jnp.int32),
            pltpu.VMEM((1, 16), jnp.int32),
            pltpu.VMEM((1, 16), jnp.int32),
            pltpu.VMEM((2, 16), F32),
            pltpu.VMEM((4 * ROWS, 16), BF),
            dma((NB, 6)),
            dma((NB,)),
            dma((6,)),
            dma((2, 3, NB)),
            dma((2, 3, NB)),
            dma((7,)),
            dma((8,)),
            dma((7,)),
            dma((8,)),
            dma((4,)),
            dma((NB, 4)),
            dma(()),
        ],
        compiler_params=pltpu.CompilerParams(
            collective_id=0, has_side_effects=True, vmem_limit_bytes=60 * 2**20
        ),
        name="relax",
    )(
        tiled(load_current), tiled(diagonal), start_field, tiled(start_field), blocks, multipliers,
        active_rows, contact_len.T, contact_peer.T, port_row, port_col, port_current[0],
    )


def solution(mesh):
    check_order()
    in_specs = (
        P("sub", None, "tile", None),
        P("sub", None, "tile", None),
        P("sub", None, "tile", None),
        P("sub", None, None, None, None, None),
        P("sub", None, "tile", None),
        P(),
        P(),
        P(),
        P("sub", None),
        P("sub", None),
        P("sub", None, None),
    )
    out_specs = (P("sub", None, "tile", None), P("sub", None, "tile", None))
    return jax.shard_map(
        per_device, mesh=mesh, in_specs=in_specs, out_specs=out_specs, check_vma=False
    )
```

```python
import functools

import jax
import jax.numpy as jnp
from jax import lax
from jax.experimental import pallas as pl
from jax.experimental.pallas import tpu as pltpu
from jax.sharding import PartitionSpec as P

MESH = pl.DeviceIdType.MESH
BF = jnp.bfloat16
F32 = jnp.float32
NB = 16
ROWS = 64
EARLY = 5

RUNS = (
    (0, 0, 1, 15),
    (1, 0, 1, 3),
    (0, 15, 1, 1),
    (1, 3, 1, 6),
    (1, 15, -1, 3),
    (1, 9, 1, 4),
    (2, 15, 1, 1),
    (2, 0, 1, 15),
)
ORDER = [(s, k0 + d * i) for s, k0, d, n in RUNS for i in range(n)]
TOTAL = len(ORDER)
AT = {entry: e for e, entry in enumerate(ORDER)}
AT_INFLOW = AT[(0, 15)]
AT_FAR = AT[(2, 15)]


def check_order():
    assert sorted(ORDER) == [(s, k) for s in range(3) for k in range(NB)]
    for s, k in ORDER:
        if s:
            for j in (k - 1, k, k + 1):
                if 0 <= j < NB:
                    assert AT[(s - 1, j)] + 2 <= AT[(s, k)]


def entry_of(e):
    sweep = jnp.int32(RUNS[0][0])
    block = RUNS[0][1] + RUNS[0][2] * e
    start = RUNS[0][3]
    for s, k0, d, n in RUNS[1:]:
        later = e >= start
        sweep = jnp.where(later, s, sweep)
        block = jnp.where(later, k0 + d * (e - start), block)
        start += n
    return sweep, block


def body(
    load_hbm, diag_hbm, start_hbm, edge_hbm, block_hbm, mult_hbm, active_hbm,
    len_hbm, peer_hbm, prow_hbm, pcol_hbm, pcur_hbm,
    out_ref, next_ref,
    field, src, diag, stage, upper, lower, lhs,
    held, far, inflow, part, part_in, end_in,
    peers, lens, cpeer, prow, pcol, pcur, weights, active_ref,
    in_sem, b_sem, small_sem, hs_sem, hr_sem, s1_sem, r1_sem, s2_sem, r2_sem, p_sem,
):
    sub = lax.axis_index("sub")
    tile = lax.axis_index("tile")
    last_tile = lax.axis_size("tile") - 1
    core = lax.rem(sub, 2)
    place = sub // 2
    places = lax.axis_size("sub") // 2
    partner = place * 2 + (1 - core)
    first_row = tile * ROWS
    above = lax.rem(tile + last_tile, last_tile + 1)
    below = lax.rem(tile + 1, last_tile + 1)
    line_above = jnp.where(tile > 0, ROWS + 8, ROWS + 9)
    line_below = jnp.where(tile < last_tile, 7, 6)

    def inputs_of(j):
        t = 2 * j
        copies = []
        for c in range(2):
            for h in range(2):
                copies.append(
                    pltpu.make_async_copy(
                        start_hbm.at[0, c, :, pl.ds(pl.multiple_of((t + h) * 128, 128), 128)],
                        field.at[0, c, t + h + 1, pl.ds(8, ROWS), :],
                        in_sem.at[j, 2 * c + h],
                    )
                )
        copies.append(
            pltpu.make_async_copy(
                load_hbm.at[:, :, pl.ds(t, 2)], src.at[:, :, pl.ds(t, 2)], in_sem.at[j, 4]
            )
        )
        copies.append(
            pltpu.make_async_copy(
                diag_hbm.at[:, :, pl.ds(t, 2)], diag.at[:, :, pl.ds(t, 2)], in_sem.at[j, 5]
            )
        )
        return copies

    def blocks_of(j):
        return pltpu.make_async_copy(block_hbm.at[j], stage.at[j], b_sem.at[j])

    def issue(j):
        for copy in inputs_of(j):
            copy.start()
        blocks_of(j).start()

    small = [
        pltpu.make_async_copy(a, b, small_sem.at[i])
        for i, (a, b) in enumerate(
            (
                (len_hbm, lens), (peer_hbm, cpeer), (prow_hbm, prow),
                (pcol_hbm, pcol), (pcur_hbm, pcur), (active_hbm, active_ref),
            )
        )
    ]
    own_mult = pltpu.make_async_copy(mult_hbm.at[0], held.at[place], small_sem.at[6])

    def edge_copy(side, s, k):
        t = 2 * k + 1
        row, there, to = ((8, line_above, above), (ROWS + 7, line_below, below))[side]
        return pltpu.make_async_remote_copy(
            src_ref=field.at[s, :, pl.ds(t, 2), pl.ds(row, 1), :],
            dst_ref=field.at[s, :, pl.ds(t, 2), pl.ds(there, 1), :],
            send_sem=hs_sem.at[side, s],
            recv_sem=hr_sem.at[side, s, k],
            device_id=(sub, to),
            device_id_type=MESH,
        )

    def first_edge(side):
        group, line, there, to = ((0, 0, line_above, above), (7, 7, line_below, below))[side]
        return pltpu.make_async_remote_copy(
            src_ref=edge_hbm.at[:, group, :, pl.ds(line, 1), :],
            dst_ref=field.at[0, :, pl.ds(1, 2 * NB), pl.ds(there, 1), :],
            send_sem=hs_sem.at[side, 0],
            recv_sem=hr_sem.at[side, 0, 0],
            device_id=(sub, to),
            device_id_type=MESH,
        )

    def spread(source, target, send, recv, offset, slot):
        to = lax.rem(place + offset, places)
        return pltpu.make_async_remote_copy(
            src_ref=source,
            dst_ref=target.at[slot],
            send_sem=send.at[offset - 1],
            recv_sem=recv.at[slot],
            device_id=(to * 2 + core, tile),
            device_id_type=MESH,
        )

    def to_partner(source, target, which):
        return pltpu.make_async_remote_copy(
            src_ref=source,
            dst_ref=target,
            send_sem=p_sem.at[2 * which],
            recv_sem=p_sem.at[2 * which + 1],
            device_id=(partner, tile),
            device_id_type=MESH,
        )

    def far_source():
        return out_ref.at[:, :, 2 * NB - 1]

    for copy in small:
        copy.start()
    for j in range(2):
        issue(j)
    own_mult.start()
    barrier = pltpu.get_barrier_semaphore()
    for offset in range(1, 8):
        to = lax.rem(place + offset, places)
        pl.semaphore_signal(barrier, inc=1, device_id=(to * 2 + core, tile), device_id_type=MESH)
    pl.semaphore_signal(barrier, inc=1, device_id=(partner, tile), device_id_type=MESH)

    pl.semaphore_signal(barrier, inc=1, device_id=(sub, above), device_id_type=MESH)
    pl.semaphore_signal(barrier, inc=1, device_id=(sub, below), device_id_type=MESH)

    @pl.loop(2, NB)
    def _(j):
        issue(j)

    for s in range(3):
        for c in range(2):
            for t in (0, 2 * NB + 1):
                field[s, c, t, 8 : ROWS + 8, :] = jnp.zeros((ROWS, 128), F32)

    @pl.when(tile == 0)
    def _():
        for s in range(3):
            field[s, :, :, 7:8, :] = jnp.zeros((2, 2 * NB + 2, 1, 128), F32)

    @pl.when(tile == last_tile)
    def _():
        for s in range(3):
            field[s, :, :, ROWS + 8 : ROWS + 9, :] = jnp.zeros((2, 2 * NB + 2, 1, 128), F32)

    for copy in small:
        copy.wait()
    active = active_ref[sub]
    length = lens[...]
    ends = length
    depth = lax.broadcasted_iota(jnp.int32, length.shape, 0)
    for step in (1, 2, 4):
        ends = ends + jnp.where(depth >= step, pltpu.roll(ends, step, 0), 0)
    starts = ends - length
    named = cpeer[...]
    line16 = lax.broadcasted_iota(jnp.int32, (ROWS, 16), 0) + first_row
    found = jnp.zeros((ROWS, 16), jnp.int32)
    for c in range(8):
        inside = (line16 >= starts[c : c + 1, :]) & (line16 < ends[c : c + 1, :])
        found = found + jnp.where(inside, named[c : c + 1, :], 0)
    peers[...] = found.astype(F32)
    rows_hot = (prow[...] == line16).astype(F32)
    for c in range(2):
        weighted = rows_hot * pcur[c : c + 1, :]
        top = weighted.astype(BF)
        weights[c * ROWS : (c + 1) * ROWS, :] = top
        weights[(2 + c) * ROWS : (3 + c) * ROWS, :] = (weighted - top.astype(F32)).astype(BF)
    eye = lax.broadcasted_iota(jnp.int32, (16, 16), 0) == lax.broadcasted_iota(jnp.int32, (16, 16), 1)
    col = jnp.sum(jnp.where(eye, pcol[...].astype(F32), 0.0), axis=1, keepdims=True)

    def line_mask():
        line = lax.broadcasted_iota(jnp.int32, (ROWS, 128), 0) + first_row
        return (line < active).astype(F32)

    def split(j):
        for q in range(4):
            v = stage[j, pl.ds(q, 512, stride=4), :].T
            top = v.astype(BF)
            upper[j, q * 128 : (q + 1) * 128, :] = top
            lower[j, q * 128 : (q + 1) * 128, :] = (v - top.astype(F32)).astype(BF)

    def await_inputs(j):
        for copy in inputs_of(j):
            copy.wait()
        blocks_of(j).wait()

    def prepare(j):
        mask = line_mask()
        at = lax.broadcasted_iota(jnp.int32, (16, 256), 1).astype(F32) + (j * 256).astype(F32)
        cols_hot = ((at >= col) & (at < col + 128.0)).astype(F32).astype(BF)
        fed = jnp.dot(weights[...], cols_hot, preferred_element_type=F32)
        for c in range(2):
            for h in range(2):
                t = 2 * j + h
                field[0, c, t + 1, 8 : ROWS + 8, :] = field[0, c, t + 1, 8 : ROWS + 8, :] * mask
                add = (
                    fed[c * ROWS : (c + 1) * ROWS, h * 128 : (h + 1) * 128]
                    + fed[(2 + c) * ROWS : (3 + c) * ROWS, h * 128 : (h + 1) * 128]
                )
                src[c, :, t] = src[c, :, t] + add.reshape(8, 8, 128)

    def residual(s, k, slot):
        lane = lax.broadcasted_iota(jnp.int32, (ROWS, 128), 1)
        t = 2 * k + 1
        mid, beside = [], []
        for c in range(2):
            tiles = [field[s, c, t + o, 8 : ROWS + 8, :] for o in (-1, 0, 1, 2)]
            right = [pltpu.roll(tiles[i], 1, 1) for i in (0, 1, 2)]
            left = [pltpu.roll(tiles[i], 127, 1) for i in (1, 2, 3)]
            for h in range(2):
                total = (
                    field[s, c, t + h, 7 : ROWS + 7, :]
                    + field[s, c, t + h, 9 : ROWS + 9, :]
                    + jnp.where(lane == 0, right[h], right[h + 1])
                    + jnp.where(lane == 127, left[h + 1], left[h])
                )
                mid.append(tiles[1 + h])
                beside.append(total)
        for h in range(2):
            d0 = diag[0, :, 2 * k + h].reshape(ROWS, 128)
            d1 = diag[1, :, 2 * k + h].reshape(ROWS, 128)
            f0, f1 = mid[h], mid[2 + h]
            s0 = src[0, :, 2 * k + h].reshape(ROWS, 128)
            s1 = src[1, :, 2 * k + h].reshape(ROWS, 128)
            r0 = s0 - (d0 * f0 - d1 * f1 - beside[h])
            r1 = s1 - (d0 * f1 + d1 * f0 - beside[2 + h])
            for d, r in enumerate((r0, r1)):
                q = 2 * h + d
                top = r.astype(BF)
                lhs[slot, 0:ROWS, q * 128 : (q + 1) * 128] = top
                lhs[slot, ROWS : 2 * ROWS, q * 128 : (q + 1) * 128] = (r - top.astype(F32)).astype(BF)

    def relax(s, k, slot, final=None):
        both = lhs[slot]
        p = jnp.dot(both, upper[k], preferred_element_type=F32)
        q = jnp.dot(both[:ROWS], lower[k], preferred_element_type=F32)
        z = p[:ROWS] + p[ROWS:] + q
        mask = line_mask()
        fresh = []
        for c in range(2):
            for h in range(2):
                a = c * 256 + h * 128
                fresh.append(mask * (field[s, c, 2 * k + 1 + h, 8 : ROWS + 8, :] + z[:, a : a + 128]))

        def keep():
            for c in range(2):
                for h in range(2):
                    field[s + 1, c, 2 * k + 1 + h, 8 : ROWS + 8, :] = fresh[2 * c + h]

        def give():
            for c in range(2):
                for h in range(2):
                    out_ref[c, :, 2 * k + h] = fresh[2 * c + h].reshape(8, 8, 128)

        if final is None:
            pl.when(s < 2)(keep)
            pl.when(s == 2)(give)
        elif final:
            give()
        else:
            keep()

    def send_edges(s, k):
        edge_copy(0, s, k).start()
        edge_copy(1, s, k).start()

    def await_edges(s, k):
        edge_copy(0, s, k).wait_recv()
        edge_copy(1, s, k).wait_recv()

    def column(which):
        lane = lax.broadcasted_iota(jnp.int32, (ROWS, 16), 1)
        return jnp.sum(jnp.where(lane == which, peers[...], 0.0), axis=1, keepdims=True)

    await_inputs(0)
    split(0)

    pl.semaphore_wait(barrier, 10)
    first_edge(0).start()
    first_edge(1).start()

    for offset in range(1, 8):
        spread(mult_hbm.at[0], held, s1_sem, r1_sem, offset, place).start()

    @pl.loop(1, EARLY)
    def _(j):
        await_inputs(j)
        split(j)

    @pl.loop(0, EARLY)
    def _(j):
        prepare(j)

    own_mult.wait()
    for c in range(2):
        src[c, :, 0] = src[c, :, 0] - held[place, c].reshape(8, 8, 128)

    for side, row, line in ((0, ROWS + 8, first_row + ROWS), (1, 7, first_row - 1)):
        first_edge(side).wait_recv()
        scale = jnp.where(line < active, 1.0, 0.0)
        for c in range(2):
            field[0, c, 1 : 2 * NB + 1, row : row + 1, :] = (
                field[0, c, 1 : 2 * NB + 1, row : row + 1, :] * scale
            )

    residual(0, 0, 0)

    @pl.loop(0, NB - EARLY)
    def _(e):
        await_inputs(e + EARLY)
        slot = lax.rem(e, 2)
        split(e + EARLY)
        residual(0, e + 1, 1 - slot)
        relax(0, e, slot, False)
        prepare(e + EARLY)
        send_edges(1, e)

    def later(e, carry):
        s, k, s2, k2 = carry

        @pl.when(e + 1 == AT_INFLOW - 3)
        def _():
            for offset in range(1, 8):
                j = lax.rem(place + offset, places)
                spread(mult_hbm.at[0], held, s1_sem, r1_sem, offset, j).wait_recv()
            inflow[...] = jnp.zeros_like(inflow)
            part[...] = jnp.zeros_like(part)

            @pl.loop(0, 8)
            def _(j):
                seen = column(2 * j + core)
                mine = seen == sub.astype(F32)
                theirs = seen == partner.astype(F32)
                for c in range(2):
                    v = held[j, c]
                    inflow[c] = inflow[c] + jnp.where(mine, v, 0.0)
                    part[0, c] = part[0, c] + jnp.where(theirs, v, 0.0)

            to_partner(part.at[0], part_in, 0).start()

        @pl.when(e + 1 == AT_INFLOW)
        def _():
            to_partner(part.at[0], part_in, 0).wait_recv()
            for c in range(2):
                total = inflow[c] + part_in[c]
                src[c, :, 2 * NB - 1] = src[c, :, 2 * NB - 1] + total.reshape(8, 8, 128)

        @pl.when(s2 > 0)
        def _():
            await_edges(s2, k2)

        slot = lax.rem(e, 2)
        s3, k3 = entry_of(e + 2)
        residual(s2, k2, 1 - slot)
        relax(s, k, slot)

        @pl.when(s < 2)
        def _():
            send_edges(s + 1, k)

        @pl.when(e == AT_FAR)
        def _():
            for offset in range(1, 8):
                spread(far_source(), far, s2_sem, r2_sem, offset, place).start()

        return s2, k2, s3, k3

    first = NB - EARLY
    lax.fori_loop(first, TOTAL - 1, later, (*entry_of(jnp.int32(first)), *entry_of(jnp.int32(first + 1))))
    s, k = ORDER[-1]
    relax(s, k, (TOTAL - 1) % 2, True)

    own_peer = column(sub)
    their_peer = column(partner)
    far[place] = out_ref[:, :, 2 * NB - 1]
    for offset in range(1, 8):
        j = lax.rem(place + offset, places)
        spread(far_source(), far, s2_sem, r2_sem, offset, j).wait_recv()
    for c in range(2):
        mine = jnp.zeros((ROWS, 128), F32)
        theirs = jnp.zeros((ROWS, 128), F32)
        for j in range(8):
            v = far[j, c].reshape(ROWS, 128)
            at = (2 * j + core).astype(F32)
            mine = mine + jnp.where(own_peer == at, v, 0.0)
            theirs = theirs + jnp.where(their_peer == at, v, 0.0)
        inflow[c] = mine
        part[1, c] = theirs
    to_partner(part.at[1], end_in, 1).start()
    to_partner(part.at[1], end_in, 1).wait_recv()
    for c in range(2):
        near = out_ref[c, :, 0].reshape(ROWS, 128)
        next_ref[0, c] = held[place, c] + (near - (inflow[c] + end_in[c]))

    for offset in range(1, 8):
        spread(mult_hbm.at[0], held, s1_sem, r1_sem, offset, place).wait_send()
        spread(far_source(), far, s2_sem, r2_sem, offset, place).wait_send()
    to_partner(part.at[0], part_in, 0).wait_send()
    to_partner(part.at[1], end_in, 1).wait_send()

    for side in range(2):
        first_edge(side).wait_send()
        row, there, to = ((8, line_above, above), (ROWS + 7, line_below, below))[side]
        for s in (1, 2):
            pltpu.make_async_remote_copy(
                src_ref=field.at[s, :, pl.ds(1, 2 * NB), pl.ds(row, 1), :],
                dst_ref=field.at[s, :, pl.ds(1, 2 * NB), pl.ds(there, 1), :],
                send_sem=hs_sem.at[side, s],
                recv_sem=hr_sem.at[side, s, 0],
                device_id=(sub, to),
                device_id_type=MESH,
            ).wait_send()


def per_device(
    load_current, diagonal, start_field, block_inverse, multipliers, active_rows,
    contact_peer, contact_len, port_row, port_col, port_current,
):
    width = load_current.shape[3]

    def tiled(x):
        return x.reshape(2, 8, 8, width // 128, 128).transpose(0, 1, 3, 2, 4)

    def stay(x):
        return pltpu.with_memory_space_constraint(x, pltpu.HBM)

    blocks = (
        block_inverse.reshape(NB, 2, 256, 2, 2, 128).transpose(0, 1, 2, 4, 3, 5).reshape(NB, 2048, 128)
    )
    hbm = pl.BlockSpec(memory_space=pltpu.HBM)
    vmem = pl.BlockSpec(memory_space=pltpu.VMEM)
    dma = pltpu.SemaphoreType.DMA
    solved, following = pl.pallas_call(
        body,
        out_shape=(
            jax.ShapeDtypeStruct((2, 8, 2 * NB, 8, 128), F32),
            jax.ShapeDtypeStruct(multipliers.shape, F32),
        ),
        in_specs=[hbm] * 12,
        out_specs=(vmem, vmem),
        scratch_shapes=[
            pltpu.VMEM((3, 2, 2 * NB + 2, ROWS + 16, 128), F32),
            pltpu.VMEM((2, 8, 2 * NB, 8, 128), F32),
            pltpu.VMEM((2, 8, 2 * NB, 8, 128), F32),
            pltpu.VMEM((NB, 2048, 128), F32),
            pltpu.VMEM((NB, 512, 512), BF),
            pltpu.VMEM((NB, 512, 512), BF),
            pltpu.VMEM((2, 2 * ROWS, 512), BF),
            pltpu.VMEM((8, 2, ROWS, 128), F32),
            pltpu.VMEM((8, 2, 8, 8, 128), F32),
            pltpu.VMEM((2, ROWS, 128), F32),
            pltpu.VMEM((2, 2, ROWS, 128), F32),
            pltpu.VMEM((2, ROWS, 128), F32),
            pltpu.VMEM((2, ROWS, 128), F32),
            pltpu.VMEM((ROWS, 16), F32),
            pltpu.VMEM((8, 16), jnp.int32),
            pltpu.VMEM((8, 16), jnp.int32),
            pltpu.VMEM((1, 16), jnp.int32),
            pltpu.VMEM((1, 16), jnp.int32),
            pltpu.VMEM((2, 16), F32),
            pltpu.VMEM((4 * ROWS, 16), BF),
            pltpu.SMEM((16,), jnp.int32),
            dma((NB, 6)),
            dma((NB,)),
            dma((7,)),
            dma((2, 3)),
            dma((2, 3, NB)),
            dma((7,)),
            dma((8,)),
            dma((7,)),
            dma((8,)),
            dma((4,)),
        ],
        compiler_params=pltpu.CompilerParams(
            collective_id=0, has_side_effects=True, vmem_limit_bytes=51 * 2**20
        ),
        name="relax",
    )(
        tiled(load_current), tiled(diagonal), start_field, tiled(start_field), blocks, stay(multipliers),
        stay(active_rows), stay(contact_len.T), stay(contact_peer.T), stay(port_row), stay(port_col),
        stay(port_current[0]),
    )
    return solved.transpose(0, 1, 3, 2, 4).reshape(load_current.shape), following


def solution(mesh):
    check_order()
    in_specs = (
        P("sub", None, "tile", None),
        P("sub", None, "tile", None),
        P("sub", None, "tile", None),
        P("sub", None, None, None, None, None),
        P("sub", None, "tile", None),
        P(),
        P(),
        P(),
        P("sub", None),
        P("sub", None),
        P("sub", None, None),
    )
    out_specs = (P("sub", None, "tile", None), P("sub", None, "tile", None))
    return jax.shard_map(
        per_device, mesh=mesh, in_specs=in_specs, out_specs=out_specs, check_vma=False
    )
```

```python
import functools

import jax
import jax.numpy as jnp
from jax import lax
from jax.experimental import pallas as pl
from jax.experimental.pallas import tpu as pltpu
from jax.sharding import PartitionSpec as P

MESH = pl.DeviceIdType.MESH
BF = jnp.bfloat16
F32 = jnp.float32
NB = 16
ROWS = 64
EARLY = 4

EVEN = ((0, 0, 0, 2), (8, 1, 0, 2), (12, 1, 14, 0), (13, 1, 8, 2), (16, 2, 0, 2))
ODD = (
    (0, 0, 1, 2), (7, 1, 1, 0), (8, 0, 15, 0), (9, 1, 3, 2), (12, 1, 15, 0),
    (13, 1, 9, 2), (16, 2, 15, 0), (17, 2, 1, 2),
)
STEPS = 24
SPLITS = (NB - EARLY) // 2
AT_INFLOW = 8
AT_FAR = 16


def static_entry(runs, m):
    first, s, k0, d = [run for run in runs if run[0] <= m][-1]
    return s, k0 + d * (m - first)


def check_order():
    order = [static_entry(r, m) for m in range(STEPS) for r in (EVEN, ODD)]
    at = {entry: e for e, entry in enumerate(order)}
    assert sorted(order) == [(s, k) for s in range(3) for k in range(NB)]
    assert order[2 * AT_INFLOW + 1] == (0, 15) and order[2 * AT_FAR + 1] == (2, 15)
    assert all(k % 2 == e % 2 for e, (s, k) in enumerate(order))
    assert all(order[e] == (0, e) for e in range(2 * SPLITS + 1))
    for s, k in order:
        if s:
            for j in (k - 1, k, k + 1):
                if 0 <= j < NB:
                    assert at[(s - 1, j)] + 2 <= at[(s, k)]


def entry_of(runs, m):
    _, s, k0, d = runs[0]
    sweep = jnp.int32(s)
    block = k0 + d * m
    for first, s, k0, d in runs[1:]:
        later = m >= first
        sweep = jnp.where(later, s, sweep)
        block = jnp.where(later, k0 + d * (m - first), block)
    return sweep, block


def body(
    load_hbm, diag_hbm, start_hbm, edge_hbm, block_hbm, mult_hbm, active_hbm,
    len_hbm, peer_hbm, prow_hbm, pcol_hbm, pcur_hbm,
    out_ref, next_ref,
    field, src, diag, stage, upper_even, lower_even, upper_odd, lower_odd, lhs_even, lhs_odd,
    held, far, inflow, part, part_in, end_in,
    peers, lens, cpeer, prow, pcol, pcur, weights, active_ref,
    in_sem, b_sem, small_sem, hs_sem, hr_sem, s1_sem, r1_sem, s2_sem, r2_sem, p_sem,
):
    sub = lax.axis_index("sub")
    tile = lax.axis_index("tile")
    last_tile = lax.axis_size("tile") - 1
    core = lax.rem(sub, 2)
    place = sub // 2
    places = lax.axis_size("sub") // 2
    partner = place * 2 + (1 - core)
    first_row = tile * ROWS
    above = lax.rem(tile + last_tile, last_tile + 1)
    below = lax.rem(tile + 1, last_tile + 1)
    line_above = jnp.where(tile > 0, ROWS + 8, ROWS + 9)
    line_below = jnp.where(tile < last_tile, 7, 6)

    def inputs_of(j):
        t = 2 * j
        copies = []
        for c in range(2):
            for h in range(2):
                copies.append(
                    pltpu.make_async_copy(
                        start_hbm.at[0, c, :, pl.ds(pl.multiple_of((t + h) * 128, 128), 128)],
                        field.at[0, c, t + h + 1, pl.ds(8, ROWS), :],
                        in_sem.at[j, 2 * c + h],
                    )
                )
        copies.append(
            pltpu.make_async_copy(
                load_hbm.at[:, :, pl.ds(t, 2)], src.at[:, :, pl.ds(t, 2)], in_sem.at[j, 4]
            )
        )
        copies.append(
            pltpu.make_async_copy(
                diag_hbm.at[:, :, pl.ds(t, 2)], diag.at[:, :, pl.ds(t, 2)], in_sem.at[j, 5]
            )
        )
        return copies

    def blocks_of(j):
        return pltpu.make_async_copy(block_hbm.at[j], stage.at[j], b_sem.at[j])

    def issue(j):
        for copy in inputs_of(j):
            copy.start()
        blocks_of(j).start()

    small = [
        pltpu.make_async_copy(a, b, small_sem.at[i])
        for i, (a, b) in enumerate(
            (
                (len_hbm, lens), (peer_hbm, cpeer), (prow_hbm, prow),
                (pcol_hbm, pcol), (pcur_hbm, pcur), (active_hbm, active_ref),
            )
        )
    ]
    own_mult = pltpu.make_async_copy(mult_hbm.at[0], held.at[place], small_sem.at[6])

    def edge_copy(side, s, k):
        t = 2 * k + 1
        row, there, to = ((8, line_above, above), (ROWS + 7, line_below, below))[side]
        return pltpu.make_async_remote_copy(
            src_ref=field.at[s, :, pl.ds(t, 2), pl.ds(row, 1), :],
            dst_ref=field.at[s, :, pl.ds(t, 2), pl.ds(there, 1), :],
            send_sem=hs_sem.at[side, s],
            recv_sem=hr_sem.at[side, s, k],
            device_id=(sub, to),
            device_id_type=MESH,
        )

    def first_edge(side):
        group, line, there, to = ((0, 0, line_above, above), (7, 7, line_below, below))[side]
        return pltpu.make_async_remote_copy(
            src_ref=edge_hbm.at[:, group, :, pl.ds(line, 1), :],
            dst_ref=field.at[0, :, pl.ds(1, 2 * NB), pl.ds(there, 1), :],
            send_sem=hs_sem.at[side, 0],
            recv_sem=hr_sem.at[side, 0, 0],
            device_id=(sub, to),
            device_id_type=MESH,
        )

    def spread(source, target, send, recv, offset, slot):
        to = lax.rem(place + offset, places)
        return pltpu.make_async_remote_copy(
            src_ref=source,
            dst_ref=target.at[slot],
            send_sem=send.at[offset - 1],
            recv_sem=recv.at[slot],
            device_id=(to * 2 + core, tile),
            device_id_type=MESH,
        )

    def to_partner(source, target, which):
        return pltpu.make_async_remote_copy(
            src_ref=source,
            dst_ref=target,
            send_sem=p_sem.at[2 * which],
            recv_sem=p_sem.at[2 * which + 1],
            device_id=(partner, tile),
            device_id_type=MESH,
        )

    def far_source():
        return field.at[3, :, 2 * NB, pl.ds(8, ROWS), :]

    for copy in small:
        copy.start()
    for j in range(2):
        issue(j)
    own_mult.start()
    barrier = pltpu.get_barrier_semaphore()
    for offset in range(1, 8):
        to = lax.rem(place + offset, places)
        pl.semaphore_signal(barrier, inc=1, device_id=(to * 2 + core, tile), device_id_type=MESH)
    pl.semaphore_signal(barrier, inc=1, device_id=(partner, tile), device_id_type=MESH)

    pl.semaphore_signal(barrier, inc=1, device_id=(sub, above), device_id_type=MESH)
    pl.semaphore_signal(barrier, inc=1, device_id=(sub, below), device_id_type=MESH)

    @pl.loop(2, NB)
    def _(j):
        issue(j)

    for s in range(3):
        for c in range(2):
            for t in (0, 2 * NB + 1):
                field[s, c, t, 8 : ROWS + 8, :] = jnp.zeros((ROWS, 128), F32)

    @pl.when(tile == 0)
    def _():
        for s in range(3):
            field[s, :, :, 7:8, :] = jnp.zeros((2, 2 * NB + 2, 1, 128), F32)

    @pl.when(tile == last_tile)
    def _():
        for s in range(3):
            field[s, :, :, ROWS + 8 : ROWS + 9, :] = jnp.zeros((2, 2 * NB + 2, 1, 128), F32)

    for copy in small:
        copy.wait()
    active = active_ref[sub]
    length = lens[...]
    ends = length
    depth = lax.broadcasted_iota(jnp.int32, length.shape, 0)
    for step in (1, 2, 4):
        ends = ends + jnp.where(depth >= step, pltpu.roll(ends, step, 0), 0)
    starts = ends - length
    named = cpeer[...]
    line16 = lax.broadcasted_iota(jnp.int32, (ROWS, 16), 0) + first_row
    found = jnp.zeros((ROWS, 16), jnp.int32)
    for c in range(8):
        inside = (line16 >= starts[c : c + 1, :]) & (line16 < ends[c : c + 1, :])
        found = found + jnp.where(inside, named[c : c + 1, :], 0)
    peers[...] = found.astype(F32)
    rows_hot = (prow[...] == line16).astype(F32)
    for c in range(2):
        weighted = rows_hot * pcur[c : c + 1, :]
        top = weighted.astype(BF)
        weights[c * ROWS : (c + 1) * ROWS, :] = top
        weights[(2 + c) * ROWS : (3 + c) * ROWS, :] = (weighted - top.astype(F32)).astype(BF)
    eye = lax.broadcasted_iota(jnp.int32, (16, 16), 0) == lax.broadcasted_iota(jnp.int32, (16, 16), 1)
    col = jnp.sum(jnp.where(eye, pcol[...].astype(F32), 0.0), axis=1, keepdims=True)

    def line_mask():
        line = lax.broadcasted_iota(jnp.int32, (ROWS, 128), 0) + first_row
        return (line < active).astype(F32)

    def split(j, odd):
        upper, lower = ((upper_even, lower_even), (upper_odd, lower_odd))[odd]
        for q in range(4):
            v = stage[j, pl.ds(q, 512, stride=4), :].T
            top = v.astype(BF)
            upper[j // 2, q * 128 : (q + 1) * 128, :] = top
            lower[j // 2, q * 128 : (q + 1) * 128, :] = (v - top.astype(F32)).astype(BF)

    def await_inputs(j):
        for copy in inputs_of(j):
            copy.wait()
        blocks_of(j).wait()

    def prepare(j):
        mask = line_mask()
        at = lax.broadcasted_iota(jnp.int32, (16, 256), 1).astype(F32) + (j * 256).astype(F32)
        cols_hot = ((at >= col) & (at < col + 128.0)).astype(F32).astype(BF)
        fed = jnp.dot(weights[...], cols_hot, preferred_element_type=F32)
        for c in range(2):
            for h in range(2):
                t = 2 * j + h
                field[0, c, t + 1, 8 : ROWS + 8, :] = field[0, c, t + 1, 8 : ROWS + 8, :] * mask
                add = (
                    fed[c * ROWS : (c + 1) * ROWS, h * 128 : (h + 1) * 128]
                    + fed[(2 + c) * ROWS : (3 + c) * ROWS, h * 128 : (h + 1) * 128]
                )
                src[c, :, t] = src[c, :, t] + add.reshape(8, 8, 128)

    def residual(s, k, lhs):
        lane = lax.broadcasted_iota(jnp.int32, (ROWS, 128), 1)
        t = 2 * k + 1
        mid, beside = [], []
        for c in range(2):
            tiles = [field[s, c, t + o, 8 : ROWS + 8, :] for o in (-1, 0, 1, 2)]
            right = [pltpu.roll(tiles[i], 1, 1) for i in (0, 1, 2)]
            left = [pltpu.roll(tiles[i], 127, 1) for i in (1, 2, 3)]
            for h in range(2):
                total = (
                    field[s, c, t + h, 7 : ROWS + 7, :]
                    + field[s, c, t + h, 9 : ROWS + 9, :]
                    + jnp.where(lane == 0, right[h], right[h + 1])
                    + jnp.where(lane == 127, left[h + 1], left[h])
                )
                mid.append(tiles[1 + h])
                beside.append(total)
        for h in range(2):
            d0 = diag[0, :, 2 * k + h].reshape(ROWS, 128)
            d1 = diag[1, :, 2 * k + h].reshape(ROWS, 128)
            f0, f1 = mid[h], mid[2 + h]
            s0 = src[0, :, 2 * k + h].reshape(ROWS, 128)
            s1 = src[1, :, 2 * k + h].reshape(ROWS, 128)
            r0 = s0 - (d0 * f0 - d1 * f1 - beside[h])
            r1 = s1 - (d0 * f1 + d1 * f0 - beside[2 + h])
            for d, r in enumerate((r0, r1)):
                q = 2 * h + d
                top = r.astype(BF)
                lhs[0:ROWS, q * 128 : (q + 1) * 128] = top
                lhs[ROWS : 2 * ROWS, q * 128 : (q + 1) * 128] = (r - top.astype(F32)).astype(BF)

    def product(k, odd):
        lhs, upper, lower = ((lhs_even, upper_even, lower_even), (lhs_odd, upper_odd, lower_odd))[odd]
        both = lhs[...]
        p = jnp.dot(both, upper[k // 2], preferred_element_type=F32)
        q = jnp.dot(both[:ROWS], lower[k // 2], preferred_element_type=F32)
        return p[:ROWS] + p[ROWS:] + q

    def update(s, k, z):
        mask = line_mask()
        for c in range(2):
            for h in range(2):
                t = 2 * k + 1 + h
                a = c * 256 + h * 128
                field[s + 1, c, t, 8 : ROWS + 8, :] = mask * (
                    field[s, c, t, 8 : ROWS + 8, :] + z[:, a : a + 128]
                )

    def send_edges(s, k):
        edge_copy(0, s, k).start()
        edge_copy(1, s, k).start()

    def await_edges(s, k):
        edge_copy(0, s, k).wait_recv()
        edge_copy(1, s, k).wait_recv()

    def column(which):
        lane = lax.broadcasted_iota(jnp.int32, (ROWS, 16), 1)
        return jnp.sum(jnp.where(lane == which, peers[...], 0.0), axis=1, keepdims=True)

    await_inputs(0)
    split(0, 0)

    pl.semaphore_wait(barrier, 10)
    first_edge(0).start()
    first_edge(1).start()

    for offset in range(1, 8):
        spread(mult_hbm.at[0], held, s1_sem, r1_sem, offset, place).start()

    for j in range(1, EARLY):
        await_inputs(j)
        split(j, j % 2)

    @pl.loop(0, EARLY)
    def _(j):
        prepare(j)

    own_mult.wait()
    for c in range(2):
        src[c, :, 0] = src[c, :, 0] - held[place, c].reshape(8, 8, 128)

    for side, row, line in ((0, ROWS + 8, first_row + ROWS), (1, 7, first_row - 1)):
        first_edge(side).wait_recv()
        scale = jnp.where(line < active, 1.0, 0.0)
        for c in range(2):
            field[0, c, 1 : 2 * NB + 1, row : row + 1, :] = (
                field[0, c, 1 : 2 * NB + 1, row : row + 1, :] * scale
            )

    residual(0, 0, lhs_even)

    @pl.loop(0, SPLITS)
    def _(m):
        e = 2 * m
        await_inputs(e + EARLY)
        await_inputs(e + EARLY + 1)
        residual(0, e + 1, lhs_odd)
        z = product(e, 0)
        split(e + EARLY + 1, 1)
        prepare(e + EARLY)
        prepare(e + EARLY + 1)
        update(0, e, z)
        residual(0, e + 2, lhs_even)
        z = product(e + 1, 1)
        split(e + EARLY, 0)
        update(0, e + 1, z)
        send_edges(1, e)
        send_edges(1, e + 1)

    def later(m, carry):
        s0, k0, s1, k1, s2, k2 = carry

        @pl.when(m == AT_INFLOW - 1)
        def _():
            for offset in range(1, 8):
                j = lax.rem(place + offset, places)
                spread(mult_hbm.at[0], held, s1_sem, r1_sem, offset, j).wait_recv()
            inflow[...] = jnp.zeros_like(inflow)
            part[...] = jnp.zeros_like(part)

            @pl.loop(0, 8)
            def _(j):
                seen = column(2 * j + core)
                mine = seen == sub.astype(F32)
                theirs = seen == partner.astype(F32)
                for c in range(2):
                    v = held[j, c]
                    inflow[c] = inflow[c] + jnp.where(mine, v, 0.0)
                    part[0, c] = part[0, c] + jnp.where(theirs, v, 0.0)

            to_partner(part.at[0], part_in, 0).start()

        @pl.when(m == AT_INFLOW)
        def _():
            to_partner(part.at[0], part_in, 0).wait_recv()
            for c in range(2):
                total = inflow[c] + part_in[c]
                src[c, :, 2 * NB - 1] = src[c, :, 2 * NB - 1] + total.reshape(8, 8, 128)

        @pl.when(s1 > 0)
        def _():
            await_edges(s1, k1)

        @pl.when(s2 > 0)
        def _():
            await_edges(s2, k2)

        s3, k3 = entry_of(ODD, m + 1)
        s4, k4 = entry_of(EVEN, m + 2)
        residual(s1, k1, lhs_odd)
        update(s0, k0, product(k0, 0))
        residual(s2, k2, lhs_even)
        update(s1, k1, product(k1, 1))

        @pl.when(s0 < 2)
        def _():
            send_edges(s0 + 1, k0)

        @pl.when(s1 < 2)
        def _():
            send_edges(s1 + 1, k1)

        @pl.when(m == AT_FAR)
        def _():
            for offset in range(1, 8):
                spread(far_source(), far, s2_sem, r2_sem, offset, place).start()

        return s2, k2, s3, k3, s4, k4

    first = jnp.int32(SPLITS)
    lax.fori_loop(
        SPLITS, STEPS - 1, later,
        (*entry_of(EVEN, first), *entry_of(ODD, first), *entry_of(EVEN, first + 1)),
    )
    s, k = static_entry(ODD, STEPS - 1)
    await_edges(s, k)
    residual(s, k, lhs_odd)
    s0, k0 = static_entry(EVEN, STEPS - 1)
    update(s0, k0, product(k0, 0))
    update(s, k, product(k, 1))
    for c in range(2):
        for g in range(8):
            out_ref[c, g] = field[3, c, 1 : 2 * NB + 1, 8 * g + 8 : 8 * g + 16, :]

    own_peer = column(sub)
    their_peer = column(partner)
    far[place] = field[3, :, 2 * NB, 8 : ROWS + 8, :]
    for offset in range(1, 8):
        j = lax.rem(place + offset, places)
        spread(far_source(), far, s2_sem, r2_sem, offset, j).wait_recv()
    for c in range(2):
        mine = jnp.zeros((ROWS, 128), F32)
        theirs = jnp.zeros((ROWS, 128), F32)
        for j in range(8):
            v = far[j, c]
            at = (2 * j + core).astype(F32)
            mine = mine + jnp.where(own_peer == at, v, 0.0)
            theirs = theirs + jnp.where(their_peer == at, v, 0.0)
        inflow[c] = mine
        part[1, c] = theirs
    to_partner(part.at[1], end_in, 1).start()
    to_partner(part.at[1], end_in, 1).wait_recv()
    for c in range(2):
        near = field[3, c, 1, 8 : ROWS + 8, :]
        next_ref[0, c] = held[place, c] + (near - (inflow[c] + end_in[c]))

    for offset in range(1, 8):
        spread(mult_hbm.at[0], held, s1_sem, r1_sem, offset, place).wait_send()
        spread(far_source(), far, s2_sem, r2_sem, offset, place).wait_send()
    to_partner(part.at[0], part_in, 0).wait_send()
    to_partner(part.at[1], end_in, 1).wait_send()

    for side in range(2):
        first_edge(side).wait_send()
        row, there, to = ((8, line_above, above), (ROWS + 7, line_below, below))[side]
        for s in (1, 2):
            pltpu.make_async_remote_copy(
                src_ref=field.at[s, :, pl.ds(1, 2 * NB), pl.ds(row, 1), :],
                dst_ref=field.at[s, :, pl.ds(1, 2 * NB), pl.ds(there, 1), :],
                send_sem=hs_sem.at[side, s],
                recv_sem=hr_sem.at[side, s, 0],
                device_id=(sub, to),
                device_id_type=MESH,
            ).wait_send()


def per_device(
    load_current, diagonal, start_field, block_inverse, multipliers, active_rows,
    contact_peer, contact_len, port_row, port_col, port_current,
):
    width = load_current.shape[3]

    def tiled(x):
        return x.reshape(2, 8, 8, width // 128, 128).transpose(0, 1, 3, 2, 4)

    def stay(x):
        return pltpu.with_memory_space_constraint(x, pltpu.HBM)

    blocks = (
        block_inverse.reshape(NB, 2, 256, 2, 2, 128).transpose(0, 1, 2, 4, 3, 5).reshape(NB, 2048, 128)
    )
    hbm = pl.BlockSpec(memory_space=pltpu.HBM)
    vmem = pl.BlockSpec(memory_space=pltpu.VMEM)
    dma = pltpu.SemaphoreType.DMA
    solved, following = pl.pallas_call(
        body,
        out_shape=(
            jax.ShapeDtypeStruct((2, 8, 2 * NB, 8, 128), F32),
            jax.ShapeDtypeStruct(multipliers.shape, F32),
        ),
        in_specs=[hbm] * 12,
        out_specs=(vmem, vmem),
        scratch_shapes=[
            pltpu.VMEM((4, 2, 2 * NB + 2, ROWS + 16, 128), F32),
            pltpu.VMEM((2, 8, 2 * NB, 8, 128), F32),
            pltpu.VMEM((2, 8, 2 * NB, 8, 128), F32),
            pltpu.VMEM((NB, 2048, 128), F32),
            pltpu.VMEM((NB // 2, 512, 512), BF),
            pltpu.VMEM((NB // 2, 512, 512), BF),
            pltpu.VMEM((NB // 2, 512, 512), BF),
            pltpu.VMEM((NB // 2, 512, 512), BF),
            pltpu.VMEM((2 * ROWS, 512), BF),
            pltpu.VMEM((2 * ROWS, 512), BF),
            pltpu.VMEM((8, 2, ROWS, 128), F32),
            pltpu.VMEM((8, 2, ROWS, 128), F32),
            pltpu.VMEM((2, ROWS, 128), F32),
            pltpu.VMEM((2, 2, ROWS, 128), F32),
            pltpu.VMEM((2, ROWS, 128), F32),
            pltpu.VMEM((2, ROWS, 128), F32),
            pltpu.VMEM((ROWS, 16), F32),
            pltpu.VMEM((8, 16), jnp.int32),
            pltpu.VMEM((8, 16), jnp.int32),
            pltpu.VMEM((1, 16), jnp.int32),
            pltpu.VMEM((1, 16), jnp.int32),
            pltpu.VMEM((2, 16), F32),
            pltpu.VMEM((4 * ROWS, 16), BF),
            pltpu.SMEM((16,), jnp.int32),
            dma((NB, 6)),
            dma((NB,)),
            dma((7,)),
            dma((2, 3)),
            dma((2, 3, NB)),
            dma((7,)),
            dma((8,)),
            dma((7,)),
            dma((8,)),
            dma((4,)),
        ],
        compiler_params=pltpu.CompilerParams(
            collective_id=0, has_side_effects=True, vmem_limit_bytes=51 * 2**20
        ),
        name="relax",
    )(
        tiled(load_current), tiled(diagonal), start_field, tiled(start_field), blocks, stay(multipliers),
        stay(active_rows), stay(contact_len.T), stay(contact_peer.T), stay(port_row), stay(port_col),
        stay(port_current[0]),
    )
    return solved.transpose(0, 1, 3, 2, 4).reshape(load_current.shape), following


def solution(mesh):
    check_order()
    in_specs = (
        P("sub", None, "tile", None),
        P("sub", None, "tile", None),
        P("sub", None, "tile", None),
        P("sub", None, None, None, None, None),
        P("sub", None, "tile", None),
        P(),
        P(),
        P(),
        P("sub", None),
        P("sub", None),
        P("sub", None, None),
    )
    out_specs = (P("sub", None, "tile", None), P("sub", None, "tile", None))
    return jax.shard_map(
        per_device, mesh=mesh, in_specs=in_specs, out_specs=out_specs, check_vma=False
    )
```

```python
import functools

import jax
import jax.numpy as jnp
from jax import lax
from jax.experimental import pallas as pl
from jax.experimental.pallas import tpu as pltpu
from jax.sharding import PartitionSpec as P

MESH = pl.DeviceIdType.MESH
BF = jnp.bfloat16
F32 = jnp.float32
NB = 16
ROWS = 64
EARLY = 12
FIRST = 4

EVEN = ((0, 0, 0, 2), (8, 1, 0, 2), (11, 1, 14, 0), (12, 1, 6, 2), (16, 2, 0, 2))
ODD = (
    (0, 0, 1, 2), (8, 1, 1, 2), (11, 1, 15, 0), (12, 1, 7, 2), (14, 2, 15, 0),
    (15, 1, 11, 2), (17, 2, 1, 2),
)
STEPS = 24
SPLITS = (NB - EARLY) // 2
AT_INFLOW = 7
AT_FAR = 14


def static_entry(runs, m):
    first, s, k0, d = [run for run in runs if run[0] <= m][-1]
    return s, k0 + d * (m - first)


def check_order():
    order = [static_entry(r, m) for m in range(STEPS) for r in (EVEN, ODD)]
    at = {entry: e for e, entry in enumerate(order)}
    assert sorted(order) == [(s, k) for s in range(3) for k in range(NB)]
    assert order[2 * AT_INFLOW + 1] == (0, 15) and order[2 * AT_FAR + 1] == (2, 15)
    assert all(k % 2 == e % 2 for e, (s, k) in enumerate(order))
    assert all(order[e] == (0, e) for e in range(2 * SPLITS + 1))
    sent = {}
    for m in range(STEPS):
        s, k = order[2 * m + 1]
        if s < 2:
            sent[(s, k // 2)] = m
            assert max(at[(s, k - 1)], at[(s, k)]) <= 2 * m + 1
    assert len(sent) == NB
    for s, k in order:
        if s:
            e = at[(s, k)]
            assert sent[(s - 1, k // 2)] < (e - 1) // 2
            if k % 2:
                assert (s, k) == (2, NB - 1) or at[(s, k - 1)] < e
            for j in (k - 1, k, k + 1):
                if 0 <= j < NB:
                    assert at[(s - 1, j)] + 2 <= at[(s, k)]


def entry_of(runs, m):
    _, s, k0, d = runs[0]
    sweep = jnp.int32(s)
    block = k0 + d * m
    for first, s, k0, d in runs[1:]:
        later = m >= first
        sweep = jnp.where(later, s, sweep)
        block = jnp.where(later, k0 + d * (m - first), block)
    return sweep, block


def body(
    load_hbm, diag_hbm, start_hbm, edge_hbm, block_hbm, mult_hbm, active_hbm,
    len_hbm, peer_hbm, prow_hbm, pcol_hbm, pcur_hbm,
    out_ref, next_ref,
    field, src, diag, stage, upper_even, lower_even, upper_odd, lower_odd, lhs_even, lhs_odd,
    held, far, inflow, part, part_in, end_in,
    peers, lens, cpeer, prow, pcol, pcur, weights, active_ref,
    in_sem, b_sem, small_sem, hs_sem, hr_sem, s1_sem, r1_sem, s2_sem, r2_sem, p_sem,
):
    sub = lax.axis_index("sub")
    tile = lax.axis_index("tile")
    last_tile = lax.axis_size("tile") - 1
    core = lax.rem(sub, 2)
    place = sub // 2
    places = lax.axis_size("sub") // 2
    partner = place * 2 + (1 - core)
    first_row = tile * ROWS
    above = lax.rem(tile + last_tile, last_tile + 1)
    below = lax.rem(tile + 1, last_tile + 1)
    line_above = jnp.where(tile > 0, ROWS + 8, ROWS + 9)
    line_below = jnp.where(tile < last_tile, 7, 6)

    def inputs_of(j):
        t = 2 * j
        copies = []
        for c in range(2):
            for h in range(2):
                copies.append(
                    pltpu.make_async_copy(
                        start_hbm.at[0, c, :, pl.ds(pl.multiple_of((t + h) * 128, 128), 128)],
                        field.at[0, c, t + h + 1, pl.ds(8, ROWS), :],
                        in_sem.at[j, 2 * c + h],
                    )
                )
        copies.append(
            pltpu.make_async_copy(
                load_hbm.at[:, :, pl.ds(t, 2)], src.at[:, :, pl.ds(t, 2)], in_sem.at[j, 4]
            )
        )
        copies.append(
            pltpu.make_async_copy(
                diag_hbm.at[:, :, pl.ds(t, 2)], diag.at[:, :, pl.ds(t, 2)], in_sem.at[j, 5]
            )
        )
        return copies

    def blocks_of(j):
        return pltpu.make_async_copy(block_hbm.at[j], stage.at[j], b_sem.at[j])

    def issue(j):
        for copy in inputs_of(j):
            copy.start()
        blocks_of(j).start()

    small = [
        pltpu.make_async_copy(a, b, small_sem.at[i])
        for i, (a, b) in enumerate(
            (
                (len_hbm, lens), (peer_hbm, cpeer), (prow_hbm, prow),
                (pcol_hbm, pcol), (pcur_hbm, pcur), (active_hbm, active_ref),
            )
        )
    ]
    own_mult = pltpu.make_async_copy(mult_hbm.at[0], held.at[place], small_sem.at[6])

    def edge_copy(side, s, j):
        t = 4 * j + 1
        row, there, to = ((8, line_above, above), (ROWS + 7, line_below, below))[side]
        return pltpu.make_async_remote_copy(
            src_ref=field.at[s, :, pl.ds(t, 4), pl.ds(row, 1), :],
            dst_ref=field.at[s, :, pl.ds(t, 4), pl.ds(there, 1), :],
            send_sem=hs_sem.at[side, s],
            recv_sem=hr_sem.at[side, s, j],
            device_id=(sub, to),
            device_id_type=MESH,
        )

    def first_edge(side):
        group, line, there, to = ((0, 0, line_above, above), (7, 7, line_below, below))[side]
        return pltpu.make_async_remote_copy(
            src_ref=edge_hbm.at[:, group, :, pl.ds(line, 1), :],
            dst_ref=field.at[0, :, pl.ds(1, 2 * NB), pl.ds(there, 1), :],
            send_sem=hs_sem.at[side, 0],
            recv_sem=hr_sem.at[side, 0, 0],
            device_id=(sub, to),
            device_id_type=MESH,
        )

    def spread(source, target, send, recv, offset, slot):
        to = lax.rem(place + offset, places)
        return pltpu.make_async_remote_copy(
            src_ref=source,
            dst_ref=target.at[slot],
            send_sem=send.at[offset - 1],
            recv_sem=recv.at[slot],
            device_id=(to * 2 + core, tile),
            device_id_type=MESH,
        )

    def to_partner(source, target, which):
        return pltpu.make_async_remote_copy(
            src_ref=source,
            dst_ref=target,
            send_sem=p_sem.at[2 * which],
            recv_sem=p_sem.at[2 * which + 1],
            device_id=(partner, tile),
            device_id_type=MESH,
        )

    def far_source():
        return field.at[3, :, 2 * NB, pl.ds(8, ROWS), :]

    for copy in small:
        copy.start()
    for j in range(2):
        issue(j)
    own_mult.start()
    barrier = pltpu.get_barrier_semaphore()
    for offset in range(1, 8):
        to = lax.rem(place + offset, places)
        pl.semaphore_signal(barrier, inc=1, device_id=(to * 2 + core, tile), device_id_type=MESH)
    pl.semaphore_signal(barrier, inc=1, device_id=(partner, tile), device_id_type=MESH)

    pl.semaphore_signal(barrier, inc=1, device_id=(sub, above), device_id_type=MESH)
    pl.semaphore_signal(barrier, inc=1, device_id=(sub, below), device_id_type=MESH)

    @pl.loop(2, NB)
    def _(j):
        issue(j)

    for s in range(3):
        for c in range(2):
            for t in (0, 2 * NB + 1):
                field[s, c, t, 8 : ROWS + 8, :] = jnp.zeros((ROWS, 128), F32)

    @pl.when(tile == 0)
    def _():
        for s in range(3):
            field[s, :, :, 7:8, :] = jnp.zeros((2, 2 * NB + 2, 1, 128), F32)

    @pl.when(tile == last_tile)
    def _():
        for s in range(3):
            field[s, :, :, ROWS + 8 : ROWS + 9, :] = jnp.zeros((2, 2 * NB + 2, 1, 128), F32)

    for copy in small:
        copy.wait()
    active = active_ref[sub]
    length = lens[...]
    ends = length
    depth = lax.broadcasted_iota(jnp.int32, length.shape, 0)
    for step in (1, 2, 4):
        ends = ends + jnp.where(depth >= step, pltpu.roll(ends, step, 0), 0)
    starts = ends - length
    named = cpeer[...]
    line16 = lax.broadcasted_iota(jnp.int32, (ROWS, 16), 0) + first_row
    found = jnp.zeros((ROWS, 16), jnp.int32)
    for c in range(8):
        inside = (line16 >= starts[c : c + 1, :]) & (line16 < ends[c : c + 1, :])
        found = found + jnp.where(inside, named[c : c + 1, :], 0)
    peers[...] = found.astype(F32)
    rows_hot = (prow[...] == line16).astype(F32)
    for c in range(2):
        weighted = rows_hot * pcur[c : c + 1, :]
        top = weighted.astype(BF)
        weights[c * ROWS : (c + 1) * ROWS, :] = top
        weights[(2 + c) * ROWS : (3 + c) * ROWS, :] = (weighted - top.astype(F32)).astype(BF)
    eye = lax.broadcasted_iota(jnp.int32, (16, 16), 0) == lax.broadcasted_iota(jnp.int32, (16, 16), 1)
    col = jnp.sum(jnp.where(eye, pcol[...].astype(F32), 0.0), axis=1, keepdims=True)

    def line_mask():
        line = lax.broadcasted_iota(jnp.int32, (ROWS, 128), 0) + first_row
        return (line < active).astype(F32)

    def split(j, odd):
        upper, lower = ((upper_even, lower_even), (upper_odd, lower_odd))[odd]
        for q in range(4):
            v = stage[j, pl.ds(q, 512, stride=4), :].T
            top = v.astype(BF)
            upper[j // 2, q * 128 : (q + 1) * 128, :] = top
            lower[j // 2, q * 128 : (q + 1) * 128, :] = (v - top.astype(F32)).astype(BF)

    def await_inputs(j):
        for copy in inputs_of(j):
            copy.wait()
        blocks_of(j).wait()

    def prepare(j):
        mask = line_mask()
        at = lax.broadcasted_iota(jnp.int32, (16, 256), 1).astype(F32) + (j * 256).astype(F32)
        cols_hot = ((at >= col) & (at < col + 128.0)).astype(F32).astype(BF)
        fed = jnp.dot(weights[...], cols_hot, preferred_element_type=F32)
        for c in range(2):
            for h in range(2):
                t = 2 * j + h
                field[0, c, t + 1, 8 : ROWS + 8, :] = field[0, c, t + 1, 8 : ROWS + 8, :] * mask
                add = (
                    fed[c * ROWS : (c + 1) * ROWS, h * 128 : (h + 1) * 128]
                    + fed[(2 + c) * ROWS : (3 + c) * ROWS, h * 128 : (h + 1) * 128]
                )
                src[c, :, t] = src[c, :, t] + add.reshape(8, 8, 128)

    def residual(s, k, lhs):
        lane = lax.broadcasted_iota(jnp.int32, (ROWS, 128), 1)
        t = 2 * k + 1
        mid, beside = [], []
        for c in range(2):
            tiles = [field[s, c, t + o, 8 : ROWS + 8, :] for o in (-1, 0, 1, 2)]
            right = [pltpu.roll(tiles[i], 1, 1) for i in (0, 1, 2)]
            left = [pltpu.roll(tiles[i], 127, 1) for i in (1, 2, 3)]
            for h in range(2):
                total = (
                    field[s, c, t + h, 7 : ROWS + 7, :]
                    + field[s, c, t + h, 9 : ROWS + 9, :]
                    + jnp.where(lane == 0, right[h], right[h + 1])
                    + jnp.where(lane == 127, left[h + 1], left[h])
                )
                mid.append(tiles[1 + h])
                beside.append(total)
        for h in range(2):
            d0 = diag[0, :, 2 * k + h].reshape(ROWS, 128)
            d1 = diag[1, :, 2 * k + h].reshape(ROWS, 128)
            f0, f1 = mid[h], mid[2 + h]
            s0 = src[0, :, 2 * k + h].reshape(ROWS, 128)
            s1 = src[1, :, 2 * k + h].reshape(ROWS, 128)
            r0 = s0 - (d0 * f0 - d1 * f1 - beside[h])
            r1 = s1 - (d0 * f1 + d1 * f0 - beside[2 + h])
            for d, r in enumerate((r0, r1)):
                q = 2 * h + d
                top = r.astype(BF)
                lhs[0:ROWS, q * 128 : (q + 1) * 128] = top
                lhs[ROWS : 2 * ROWS, q * 128 : (q + 1) * 128] = (r - top.astype(F32)).astype(BF)

    def product(k, odd):
        lhs, upper, lower = ((lhs_even, upper_even, lower_even), (lhs_odd, upper_odd, lower_odd))[odd]
        both = lhs[...]
        p = jnp.dot(both, upper[k // 2], preferred_element_type=F32)
        q = jnp.dot(both[:ROWS], lower[k // 2], preferred_element_type=F32)
        return p[:ROWS] + p[ROWS:] + q

    def update(s, k, z):
        mask = line_mask()
        for c in range(2):
            for h in range(2):
                t = 2 * k + 1 + h
                a = c * 256 + h * 128
                field[s + 1, c, t, 8 : ROWS + 8, :] = mask * (
                    field[s, c, t, 8 : ROWS + 8, :] + z[:, a : a + 128]
                )

    def send_edges(s, j):
        edge_copy(0, s, j).start()
        edge_copy(1, s, j).start()

    def await_edges(s, j):
        edge_copy(0, s, j).wait_recv()
        edge_copy(1, s, j).wait_recv()

    def column(which):
        lane = lax.broadcasted_iota(jnp.int32, (ROWS, 16), 1)
        return jnp.sum(jnp.where(lane == which, peers[...], 0.0), axis=1, keepdims=True)

    def split_pairs(start, stop):
        @pl.loop(start // 2, stop // 2)
        def _(i):
            await_inputs(2 * i)
            split(2 * i, 0)
            await_inputs(2 * i + 1)
            split(2 * i + 1, 1)

    split_pairs(0, FIRST)

    pl.semaphore_wait(barrier, 10)
    first_edge(0).start()
    first_edge(1).start()

    for offset in range(1, 8):
        spread(mult_hbm.at[0], held, s1_sem, r1_sem, offset, place).start()

    split_pairs(FIRST, EARLY)

    @pl.loop(0, EARLY)
    def _(j):
        prepare(j)

    own_mult.wait()
    for c in range(2):
        src[c, :, 0] = src[c, :, 0] - held[place, c].reshape(8, 8, 128)

    for side, row, line in ((0, ROWS + 8, first_row + ROWS), (1, 7, first_row - 1)):
        first_edge(side).wait_recv()
        scale = jnp.where(line < active, 1.0, 0.0)
        for c in range(2):
            field[0, c, 1 : 2 * NB + 1, row : row + 1, :] = (
                field[0, c, 1 : 2 * NB + 1, row : row + 1, :] * scale
            )

    residual(0, 0, lhs_even)

    @pl.loop(0, SPLITS)
    def _(m):
        e = 2 * m
        await_inputs(e + EARLY)
        await_inputs(e + EARLY + 1)
        residual(0, e + 1, lhs_odd)
        z = product(e, 0)
        split(e + EARLY + 1, 1)
        prepare(e + EARLY)
        prepare(e + EARLY + 1)
        update(0, e, z)
        residual(0, e + 2, lhs_even)
        z = product(e + 1, 1)
        split(e + EARLY, 0)
        update(0, e + 1, z)
        send_edges(1, m)

    def later(m, carry):
        s0, k0, s1, k1, s2, k2 = carry

        @pl.when(m == AT_INFLOW - 2)
        def _():
            for offset in range(1, 8):
                j = lax.rem(place + offset, places)
                spread(mult_hbm.at[0], held, s1_sem, r1_sem, offset, j).wait_recv()
            inflow[...] = jnp.zeros_like(inflow)
            part[...] = jnp.zeros_like(part)

            @pl.loop(0, 8)
            def _(j):
                seen = column(2 * j + core)
                mine = seen == sub.astype(F32)
                theirs = seen == partner.astype(F32)
                for c in range(2):
                    v = held[j, c]
                    inflow[c] = inflow[c] + jnp.where(mine, v, 0.0)
                    part[0, c] = part[0, c] + jnp.where(theirs, v, 0.0)

            to_partner(part.at[0], part_in, 0).start()

        @pl.when(m == AT_INFLOW)
        def _():
            to_partner(part.at[0], part_in, 0).wait_recv()
            for c in range(2):
                total = inflow[c] + part_in[c]
                src[c, :, 2 * NB - 1] = src[c, :, 2 * NB - 1] + total.reshape(8, 8, 128)

        @pl.when(m == AT_FAR)
        def _():
            await_edges(2, NB // 2 - 1)

        @pl.when((s2 > 0) & ((s2 < 2) | (k2 < NB - 2)))
        def _():
            await_edges(s2, k2 // 2)

        s3, k3 = entry_of(ODD, m + 1)
        s4, k4 = entry_of(EVEN, m + 2)
        residual(s1, k1, lhs_odd)
        update(s0, k0, product(k0, 0))
        residual(s2, k2, lhs_even)
        update(s1, k1, product(k1, 1))

        @pl.when(s1 < 2)
        def _():
            send_edges(s1 + 1, k1 // 2)

        @pl.when(m == AT_FAR)
        def _():
            for offset in range(1, 8):
                spread(far_source(), far, s2_sem, r2_sem, offset, place).start()

        return s2, k2, s3, k3, s4, k4

    first = jnp.int32(SPLITS)
    lax.fori_loop(
        SPLITS, STEPS - 1, later,
        (*entry_of(EVEN, first), *entry_of(ODD, first), *entry_of(EVEN, first + 1)),
    )
    s, k = static_entry(ODD, STEPS - 1)
    residual(s, k, lhs_odd)
    s0, k0 = static_entry(EVEN, STEPS - 1)
    update(s0, k0, product(k0, 0))
    update(s, k, product(k, 1))
    for c in range(2):
        for g in range(8):
            out_ref[c, g] = field[3, c, 1 : 2 * NB + 1, 8 * g + 8 : 8 * g + 16, :]

    own_peer = column(sub)
    their_peer = column(partner)
    far[place] = field[3, :, 2 * NB, 8 : ROWS + 8, :]
    for offset in range(1, 8):
        j = lax.rem(place + offset, places)
        spread(far_source(), far, s2_sem, r2_sem, offset, j).wait_recv()
    for c in range(2):
        mine = jnp.zeros((ROWS, 128), F32)
        theirs = jnp.zeros((ROWS, 128), F32)
        for j in range(8):
            v = far[j, c]
            at = (2 * j + core).astype(F32)
            mine = mine + jnp.where(own_peer == at, v, 0.0)
            theirs = theirs + jnp.where(their_peer == at, v, 0.0)
        inflow[c] = mine
        part[1, c] = theirs
    to_partner(part.at[1], end_in, 1).start()
    to_partner(part.at[1], end_in, 1).wait_recv()
    for c in range(2):
        near = field[3, c, 1, 8 : ROWS + 8, :]
        next_ref[0, c] = held[place, c] + (near - (inflow[c] + end_in[c]))

    for offset in range(1, 8):
        spread(mult_hbm.at[0], held, s1_sem, r1_sem, offset, place).wait_send()
        spread(far_source(), far, s2_sem, r2_sem, offset, place).wait_send()
    to_partner(part.at[0], part_in, 0).wait_send()
    to_partner(part.at[1], end_in, 1).wait_send()

    for side in range(2):
        first_edge(side).wait_send()
        row, there, to = ((8, line_above, above), (ROWS + 7, line_below, below))[side]
        for s in (1, 2):
            pltpu.make_async_remote_copy(
                src_ref=field.at[s, :, pl.ds(1, 2 * NB), pl.ds(row, 1), :],
                dst_ref=field.at[s, :, pl.ds(1, 2 * NB), pl.ds(there, 1), :],
                send_sem=hs_sem.at[side, s],
                recv_sem=hr_sem.at[side, s, 0],
                device_id=(sub, to),
                device_id_type=MESH,
            ).wait_send()


def per_device(
    load_current, diagonal, start_field, block_inverse, multipliers, active_rows,
    contact_peer, contact_len, port_row, port_col, port_current,
):
    width = load_current.shape[3]

    def tiled(x):
        return x.reshape(2, 8, 8, width // 128, 128).transpose(0, 1, 3, 2, 4)

    def stay(x):
        return pltpu.with_memory_space_constraint(x, pltpu.HBM)

    blocks = (
        block_inverse.reshape(NB, 2, 256, 2, 2, 128).transpose(0, 1, 2, 4, 3, 5).reshape(NB, 2048, 128)
    )
    hbm = pl.BlockSpec(memory_space=pltpu.HBM)
    vmem = pl.BlockSpec(memory_space=pltpu.VMEM)
    dma = pltpu.SemaphoreType.DMA
    solved, following = pl.pallas_call(
        body,
        out_shape=(
            jax.ShapeDtypeStruct((2, 8, 2 * NB, 8, 128), F32),
            jax.ShapeDtypeStruct(multipliers.shape, F32),
        ),
        in_specs=[hbm] * 12,
        out_specs=(vmem, vmem),
        scratch_shapes=[
            pltpu.VMEM((4, 2, 2 * NB + 2, ROWS + 16, 128), F32),
            pltpu.VMEM((2, 8, 2 * NB, 8, 128), F32),
            pltpu.VMEM((2, 8, 2 * NB, 8, 128), F32),
            pltpu.VMEM((NB, 2048, 128), F32),
            pltpu.VMEM((NB // 2, 512, 512), BF),
            pltpu.VMEM((NB // 2, 512, 512), BF),
            pltpu.VMEM((NB // 2, 512, 512), BF),
            pltpu.VMEM((NB // 2, 512, 512), BF),
            pltpu.VMEM((2 * ROWS, 512), BF),
            pltpu.VMEM((2 * ROWS, 512), BF),
            pltpu.VMEM((8, 2, ROWS, 128), F32),
            pltpu.VMEM((8, 2, ROWS, 128), F32),
            pltpu.VMEM((2, ROWS, 128), F32),
            pltpu.VMEM((2, 2, ROWS, 128), F32),
            pltpu.VMEM((2, ROWS, 128), F32),
            pltpu.VMEM((2, ROWS, 128), F32),
            pltpu.VMEM((ROWS, 16), F32),
            pltpu.VMEM((8, 16), jnp.int32),
            pltpu.VMEM((8, 16), jnp.int32),
            pltpu.VMEM((1, 16), jnp.int32),
            pltpu.VMEM((1, 16), jnp.int32),
            pltpu.VMEM((2, 16), F32),
            pltpu.VMEM((4 * ROWS, 16), BF),
            pltpu.SMEM((16,), jnp.int32),
            dma((NB, 6)),
            dma((NB,)),
            dma((7,)),
            dma((2, 3)),
            dma((2, 3, NB // 2)),
            dma((7,)),
            dma((8,)),
            dma((7,)),
            dma((8,)),
            dma((4,)),
        ],
        compiler_params=pltpu.CompilerParams(
            collective_id=0, has_side_effects=True, vmem_limit_bytes=51 * 2**20
        ),
        name="relax",
    )(
        tiled(load_current), tiled(diagonal), start_field, tiled(start_field), blocks, stay(multipliers),
        stay(active_rows), stay(contact_len.T), stay(contact_peer.T), stay(port_row), stay(port_col),
        stay(port_current[0]),
    )
    return solved.transpose(0, 1, 3, 2, 4).reshape(load_current.shape), following


def solution(mesh):
    check_order()
    in_specs = (
        P("sub", None, "tile", None),
        P("sub", None, "tile", None),
        P("sub", None, "tile", None),
        P("sub", None, None, None, None, None),
        P("sub", None, "tile", None),
        P(),
        P(),
        P(),
        P("sub", None),
        P("sub", None),
        P("sub", None, None),
    )
    out_specs = (P("sub", None, "tile", None), P("sub", None, "tile", None))
    return jax.shard_map(
        per_device, mesh=mesh, in_specs=in_specs, out_specs=out_specs, check_vma=False
    )
```

```python
import functools

import jax
import jax.numpy as jnp
from jax import lax
from jax.experimental import pallas as pl
from jax.experimental.pallas import tpu as pltpu
from jax.sharding import PartitionSpec as P

MESH = pl.DeviceIdType.MESH
BF = jnp.bfloat16
F32 = jnp.float32
NB = 16
ROWS = 64
EARLY = 12
FIRST = 2

EVEN = (
    (0, 0, 0, 2), (4, 0, 14, 0), (5, 0, 8, 2), (8, 1, 0, 0), (9, 1, 14, 0), (10, 1, 2, 2),
    (16, 2, 0, 2),
)
ODD = (
    (0, 0, 1, 2), (4, 0, 15, 0), (5, 0, 9, 2), (8, 1, 1, 0), (9, 1, 15, 0), (10, 1, 3, 2),
    (13, 2, 15, 0), (14, 1, 9, 2), (17, 2, 1, 2),
)
STEPS = 24
SPLITS = (NB - EARLY) // 2
AT_INFLOW = 4
AT_FAR = 13


def static_entry(runs, m):
    first, s, k0, d = [run for run in runs if run[0] <= m][-1]
    return s, k0 + d * (m - first)


def check_order():
    order = [static_entry(r, m) for m in range(STEPS) for r in (EVEN, ODD)]
    at = {entry: e for e, entry in enumerate(order)}
    assert sorted(order) == [(s, k) for s in range(3) for k in range(NB)]
    assert order[2 * AT_INFLOW + 1] == (0, 15) and order[2 * AT_FAR + 1] == (2, 15)
    assert all(k % 2 == e % 2 for e, (s, k) in enumerate(order))
    assert all(order[e] == (0, e) for e in range(2 * SPLITS + 1))
    sent = {}
    for m in range(STEPS):
        s, k = order[2 * m + 1]
        if s < 2:
            sent[(s, k // 2)] = m
            assert max(at[(s, k - 1)], at[(s, k)]) <= 2 * m + 1
    assert len(sent) == NB
    for s, k in order:
        if s:
            e = at[(s, k)]
            assert sent[(s - 1, k // 2)] < (e - 1) // 2
            if k % 2:
                assert (s, k) == (2, NB - 1) or at[(s, k - 1)] < e
            for j in (k - 1, k, k + 1):
                if 0 <= j < NB:
                    assert at[(s - 1, j)] + 2 <= at[(s, k)]


def entry_of(runs, m):
    _, s, k0, d = runs[0]
    sweep = jnp.int32(s)
    block = k0 + d * m
    for first, s, k0, d in runs[1:]:
        later = m >= first
        sweep = jnp.where(later, s, sweep)
        block = jnp.where(later, k0 + d * (m - first), block)
    return sweep, block


def body(
    load_hbm, diag_hbm, start_hbm, edge_hbm, block_hbm, mult_hbm, active_hbm,
    len_hbm, peer_hbm, prow_hbm, pcol_hbm, pcur_hbm,
    out_ref, next_ref,
    field, src, diag, stage, upper_even, lower_even, upper_odd, lower_odd, lhs_even, lhs_odd,
    held, far, inflow, part, part_in, end_in,
    peers, lens, cpeer, prow, pcol, pcur, weights, active_ref,
    in_sem, b_sem, small_sem, hs_sem, hr_sem, s1_sem, r1_sem, s2_sem, r2_sem, p_sem,
):
    sub = lax.axis_index("sub")
    tile = lax.axis_index("tile")
    last_tile = lax.axis_size("tile") - 1
    core = lax.rem(sub, 2)
    place = sub // 2
    places = lax.axis_size("sub") // 2
    partner = place * 2 + (1 - core)
    first_row = tile * ROWS
    above = lax.rem(tile + last_tile, last_tile + 1)
    below = lax.rem(tile + 1, last_tile + 1)
    line_above = jnp.where(tile > 0, ROWS + 8, ROWS + 9)
    line_below = jnp.where(tile < last_tile, 7, 6)

    def inputs_of(j):
        t = 2 * j
        copies = []
        for c in range(2):
            for h in range(2):
                copies.append(
                    pltpu.make_async_copy(
                        start_hbm.at[0, c, :, pl.ds(pl.multiple_of((t + h) * 128, 128), 128)],
                        field.at[0, c, t + h + 1, pl.ds(8, ROWS), :],
                        in_sem.at[j, 2 * c + h],
                    )
                )
        copies.append(
            pltpu.make_async_copy(
                load_hbm.at[:, :, pl.ds(t, 2)], src.at[:, :, pl.ds(t, 2)], in_sem.at[j, 4]
            )
        )
        copies.append(
            pltpu.make_async_copy(
                diag_hbm.at[:, :, pl.ds(t, 2)], diag.at[:, :, pl.ds(t, 2)], in_sem.at[j, 5]
            )
        )
        return copies

    def blocks_of(j):
        return pltpu.make_async_copy(block_hbm.at[j], stage.at[j], b_sem.at[j])

    def issue(j):
        for copy in inputs_of(j):
            copy.start()
        blocks_of(j).start()

    small = [
        pltpu.make_async_copy(a, b, small_sem.at[i])
        for i, (a, b) in enumerate(
            (
                (len_hbm, lens), (peer_hbm, cpeer), (prow_hbm, prow),
                (pcol_hbm, pcol), (pcur_hbm, pcur), (active_hbm, active_ref),
            )
        )
    ]
    own_mult = pltpu.make_async_copy(mult_hbm.at[0], held.at[place], small_sem.at[6])

    def edge_copy(side, s, j):
        t = 4 * j + 1
        row, there, to = ((8, line_above, above), (ROWS + 7, line_below, below))[side]
        return pltpu.make_async_remote_copy(
            src_ref=field.at[s, :, pl.ds(t, 4), pl.ds(row, 1), :],
            dst_ref=field.at[s, :, pl.ds(t, 4), pl.ds(there, 1), :],
            send_sem=hs_sem.at[side, s],
            recv_sem=hr_sem.at[side, s, j],
            device_id=(sub, to),
            device_id_type=MESH,
        )

    def first_edge(side):
        group, line, there, to = ((0, 0, line_above, above), (7, 7, line_below, below))[side]
        return pltpu.make_async_remote_copy(
            src_ref=edge_hbm.at[:, group, :, pl.ds(line, 1), :],
            dst_ref=field.at[0, :, pl.ds(1, 2 * NB), pl.ds(there, 1), :],
            send_sem=hs_sem.at[side, 0],
            recv_sem=hr_sem.at[side, 0, 0],
            device_id=(sub, to),
            device_id_type=MESH,
        )

    def spread(source, target, send, recv, offset, slot):
        to = lax.rem(place + offset, places)
        return pltpu.make_async_remote_copy(
            src_ref=source,
            dst_ref=target.at[slot],
            send_sem=send.at[offset - 1],
            recv_sem=recv.at[slot],
            device_id=(to * 2 + core, tile),
            device_id_type=MESH,
        )

    def to_partner(source, target, which):
        return pltpu.make_async_remote_copy(
            src_ref=source,
            dst_ref=target,
            send_sem=p_sem.at[2 * which],
            recv_sem=p_sem.at[2 * which + 1],
            device_id=(partner, tile),
            device_id_type=MESH,
        )

    def far_source():
        return field.at[3, :, 2 * NB, pl.ds(8, ROWS), :]

    barrier = pltpu.get_barrier_semaphore()
    for offset in range(1, 8):
        to = lax.rem(place + offset, places)
        pl.semaphore_signal(barrier, inc=1, device_id=(to * 2 + core, tile), device_id_type=MESH)
    pl.semaphore_signal(barrier, inc=1, device_id=(partner, tile), device_id_type=MESH)

    pl.semaphore_signal(barrier, inc=1, device_id=(sub, above), device_id_type=MESH)
    pl.semaphore_signal(barrier, inc=1, device_id=(sub, below), device_id_type=MESH)

    for copy in small:
        copy.start()
    for j in range(2):
        issue(j)
    own_mult.start()
    @pl.loop(2, NB)
    def _(j):
        issue(j)

    for s in range(3):
        for c in range(2):
            for t in (0, 2 * NB + 1):
                field[s, c, t, 8 : ROWS + 8, :] = jnp.zeros((ROWS, 128), F32)

    @pl.when(tile == 0)
    def _():
        for s in range(3):
            field[s, :, :, 7:8, :] = jnp.zeros((2, 2 * NB + 2, 1, 128), F32)

    @pl.when(tile == last_tile)
    def _():
        for s in range(3):
            field[s, :, :, ROWS + 8 : ROWS + 9, :] = jnp.zeros((2, 2 * NB + 2, 1, 128), F32)

    for copy in small:
        copy.wait()
    active = active_ref[sub]
    length = lens[...]
    ends = length
    depth = lax.broadcasted_iota(jnp.int32, length.shape, 0)
    for step in (1, 2, 4):
        ends = ends + jnp.where(depth >= step, pltpu.roll(ends, step, 0), 0)
    starts = ends - length
    named = cpeer[...]
    line16 = lax.broadcasted_iota(jnp.int32, (ROWS, 16), 0) + first_row
    found = jnp.zeros((ROWS, 16), jnp.int32)
    for c in range(8):
        inside = (line16 >= starts[c : c + 1, :]) & (line16 < ends[c : c + 1, :])
        found = found + jnp.where(inside, named[c : c + 1, :], 0)
    peers[...] = found.astype(F32)
    rows_hot = (prow[...] == line16).astype(F32)
    for c in range(2):
        weighted = rows_hot * pcur[c : c + 1, :]
        top = weighted.astype(BF)
        weights[c * ROWS : (c + 1) * ROWS, :] = top
        weights[(2 + c) * ROWS : (3 + c) * ROWS, :] = (weighted - top.astype(F32)).astype(BF)
    eye = lax.broadcasted_iota(jnp.int32, (16, 16), 0) == lax.broadcasted_iota(jnp.int32, (16, 16), 1)
    col = jnp.sum(jnp.where(eye, pcol[...].astype(F32), 0.0), axis=1, keepdims=True)

    def line_mask():
        line = lax.broadcasted_iota(jnp.int32, (ROWS, 128), 0) + first_row
        return (line < active).astype(F32)

    def split(j, odd):
        upper, lower = ((upper_even, lower_even), (upper_odd, lower_odd))[odd]
        for q in range(4):
            v = stage[j, pl.ds(q, 512, stride=4), :].T
            top = v.astype(BF)
            upper[j // 2, q * 128 : (q + 1) * 128, :] = top
            lower[j // 2, q * 128 : (q + 1) * 128, :] = (v - top.astype(F32)).astype(BF)

    def await_inputs(j):
        for copy in inputs_of(j):
            copy.wait()
        blocks_of(j).wait()

    def prepare(j):
        mask = line_mask()
        at = lax.broadcasted_iota(jnp.int32, (16, 256), 1).astype(F32) + (j * 256).astype(F32)
        cols_hot = ((at >= col) & (at < col + 128.0)).astype(F32).astype(BF)
        fed = jnp.dot(weights[...], cols_hot, preferred_element_type=F32)
        for c in range(2):
            for h in range(2):
                t = 2 * j + h
                field[0, c, t + 1, 8 : ROWS + 8, :] = field[0, c, t + 1, 8 : ROWS + 8, :] * mask
                add = (
                    fed[c * ROWS : (c + 1) * ROWS, h * 128 : (h + 1) * 128]
                    + fed[(2 + c) * ROWS : (3 + c) * ROWS, h * 128 : (h + 1) * 128]
                )
                src[c, :, t] = src[c, :, t] + add.reshape(8, 8, 128)

    def residual(s, k, lhs):
        lane = lax.broadcasted_iota(jnp.int32, (ROWS, 128), 1)
        t = 2 * k + 1
        mid, beside = [], []
        for c in range(2):
            tiles = [field[s, c, t + o, 8 : ROWS + 8, :] for o in (-1, 0, 1, 2)]
            right = [pltpu.roll(tiles[i], 1, 1) for i in (0, 1, 2)]
            left = [pltpu.roll(tiles[i], 127, 1) for i in (1, 2, 3)]
            for h in range(2):
                total = (
                    field[s, c, t + h, 7 : ROWS + 7, :]
                    + field[s, c, t + h, 9 : ROWS + 9, :]
                    + jnp.where(lane == 0, right[h], right[h + 1])
                    + jnp.where(lane == 127, left[h + 1], left[h])
                )
                mid.append(tiles[1 + h])
                beside.append(total)
        for h in range(2):
            d0 = diag[0, :, 2 * k + h].reshape(ROWS, 128)
            d1 = diag[1, :, 2 * k + h].reshape(ROWS, 128)
            f0, f1 = mid[h], mid[2 + h]
            s0 = src[0, :, 2 * k + h].reshape(ROWS, 128)
            s1 = src[1, :, 2 * k + h].reshape(ROWS, 128)
            r0 = s0 - (d0 * f0 - d1 * f1 - beside[h])
            r1 = s1 - (d0 * f1 + d1 * f0 - beside[2 + h])
            for d, r in enumerate((r0, r1)):
                q = 2 * h + d
                top = r.astype(BF)
                lhs[0:ROWS, q * 128 : (q + 1) * 128] = top
                lhs[ROWS : 2 * ROWS, q * 128 : (q + 1) * 128] = (r - top.astype(F32)).astype(BF)

    def product(k, odd):
        lhs, upper, lower = ((lhs_even, upper_even, lower_even), (lhs_odd, upper_odd, lower_odd))[odd]
        both = lhs[...]
        p = jnp.dot(both, upper[k // 2], preferred_element_type=F32)
        q = jnp.dot(both[:ROWS], lower[k // 2], preferred_element_type=F32)
        return p[:ROWS] + p[ROWS:] + q

    def update(s, k, z):
        mask = line_mask()
        for c in range(2):
            for h in range(2):
                t = 2 * k + 1 + h
                a = c * 256 + h * 128
                field[s + 1, c, t, 8 : ROWS + 8, :] = mask * (
                    field[s, c, t, 8 : ROWS + 8, :] + z[:, a : a + 128]
                )

    def send_edges(s, j):
        edge_copy(0, s, j).start()
        edge_copy(1, s, j).start()

    def await_edges(s, j):
        edge_copy(0, s, j).wait_recv()
        edge_copy(1, s, j).wait_recv()

    def column(which):
        lane = lax.broadcasted_iota(jnp.int32, (ROWS, 16), 1)
        return jnp.sum(jnp.where(lane == which, peers[...], 0.0), axis=1, keepdims=True)

    def split_pairs(start, stop):
        @pl.loop(start // 2, stop // 2)
        def _(i):
            await_inputs(2 * i)
            split(2 * i, 0)
            await_inputs(2 * i + 1)
            split(2 * i + 1, 1)

    split_pairs(0, FIRST)

    pl.semaphore_wait(barrier, 10)
    first_edge(0).start()
    first_edge(1).start()

    for offset in range(1, 8):
        spread(mult_hbm.at[0], held, s1_sem, r1_sem, offset, place).start()

    split_pairs(FIRST, EARLY)

    @pl.loop(0, EARLY)
    def _(j):
        prepare(j)

    own_mult.wait()
    for c in range(2):
        src[c, :, 0] = src[c, :, 0] - held[place, c].reshape(8, 8, 128)

    for side, row, line in ((0, ROWS + 8, first_row + ROWS), (1, 7, first_row - 1)):
        first_edge(side).wait_recv()
        scale = jnp.where(line < active, 1.0, 0.0)
        for c in range(2):
            field[0, c, 1 : 2 * NB + 1, row : row + 1, :] = (
                field[0, c, 1 : 2 * NB + 1, row : row + 1, :] * scale
            )

    residual(0, 0, lhs_even)

    @pl.loop(0, SPLITS)
    def _(m):
        e = 2 * m
        await_inputs(e + EARLY)
        await_inputs(e + EARLY + 1)
        residual(0, e + 1, lhs_odd)
        z = product(e, 0)
        split(e + EARLY + 1, 1)
        prepare(e + EARLY)
        prepare(e + EARLY + 1)
        update(0, e, z)
        residual(0, e + 2, lhs_even)
        z = product(e + 1, 1)
        split(e + EARLY, 0)
        update(0, e + 1, z)
        send_edges(1, m)

    def later(m, carry):
        s0, k0, s1, k1, s2, k2 = carry

        @pl.when(m == AT_INFLOW - 2)
        def _():
            for offset in range(1, 8):
                j = lax.rem(place + offset, places)
                spread(mult_hbm.at[0], held, s1_sem, r1_sem, offset, j).wait_recv()
            inflow[...] = jnp.zeros_like(inflow)
            part[...] = jnp.zeros_like(part)

            @pl.loop(0, 8)
            def _(j):
                seen = column(2 * j + core)
                mine = seen == sub.astype(F32)
                theirs = seen == partner.astype(F32)
                for c in range(2):
                    v = held[j, c]
                    inflow[c] = inflow[c] + jnp.where(mine, v, 0.0)
                    part[0, c] = part[0, c] + jnp.where(theirs, v, 0.0)

            to_partner(part.at[0], part_in, 0).start()

        @pl.when(m == AT_INFLOW)
        def _():
            to_partner(part.at[0], part_in, 0).wait_recv()
            for c in range(2):
                total = inflow[c] + part_in[c]
                src[c, :, 2 * NB - 1] = src[c, :, 2 * NB - 1] + total.reshape(8, 8, 128)

        @pl.when(m == AT_FAR)
        def _():
            await_edges(2, NB // 2 - 1)

        @pl.when((s2 > 0) & ((s2 < 2) | (k2 < NB - 2)))
        def _():
            await_edges(s2, k2 // 2)

        s3, k3 = entry_of(ODD, m + 1)
        s4, k4 = entry_of(EVEN, m + 2)
        residual(s1, k1, lhs_odd)
        update(s0, k0, product(k0, 0))
        residual(s2, k2, lhs_even)
        update(s1, k1, product(k1, 1))

        @pl.when(s1 < 2)
        def _():
            send_edges(s1 + 1, k1 // 2)

        @pl.when(m == AT_FAR)
        def _():
            for offset in range(1, 8):
                spread(far_source(), far, s2_sem, r2_sem, offset, place).start()

        return s2, k2, s3, k3, s4, k4

    first = jnp.int32(SPLITS)
    lax.fori_loop(
        SPLITS, STEPS - 1, later,
        (*entry_of(EVEN, first), *entry_of(ODD, first), *entry_of(EVEN, first + 1)),
    )
    s, k = static_entry(ODD, STEPS - 1)
    residual(s, k, lhs_odd)
    s0, k0 = static_entry(EVEN, STEPS - 1)
    update(s0, k0, product(k0, 0))
    update(s, k, product(k, 1))
    for c in range(2):
        for g in range(8):
            out_ref[c, g] = field[3, c, 1 : 2 * NB + 1, 8 * g + 8 : 8 * g + 16, :]

    own_peer = column(sub)
    their_peer = column(partner)
    far[place] = field[3, :, 2 * NB, 8 : ROWS + 8, :]
    mine = [jnp.zeros((ROWS, 128), F32)] * 2
    theirs = [jnp.zeros((ROWS, 128), F32)] * 2
    for offset in range(8, 0, -1):
        j = lax.rem(place + offset, places)
        if offset < 8:
            spread(far_source(), far, s2_sem, r2_sem, offset, j).wait_recv()
        at = (2 * j + core).astype(F32)
        for c in range(2):
            v = far[j, c]
            mine[c] = mine[c] + jnp.where(own_peer == at, v, 0.0)
            theirs[c] = theirs[c] + jnp.where(their_peer == at, v, 0.0)
    for c in range(2):
        inflow[c] = mine[c]
        part[1, c] = theirs[c]
    to_partner(part.at[1], end_in, 1).start()
    to_partner(part.at[1], end_in, 1).wait_recv()
    for c in range(2):
        near = field[3, c, 1, 8 : ROWS + 8, :]
        next_ref[0, c] = held[place, c] + (near - (inflow[c] + end_in[c]))

    for offset in range(1, 8):
        spread(mult_hbm.at[0], held, s1_sem, r1_sem, offset, place).wait_send()
        spread(far_source(), far, s2_sem, r2_sem, offset, place).wait_send()
    to_partner(part.at[0], part_in, 0).wait_send()
    to_partner(part.at[1], end_in, 1).wait_send()

    for side in range(2):
        first_edge(side).wait_send()
        row, there, to = ((8, line_above, above), (ROWS + 7, line_below, below))[side]
        for s in (1, 2):
            pltpu.make_async_remote_copy(
                src_ref=field.at[s, :, pl.ds(1, 2 * NB), pl.ds(row, 1), :],
                dst_ref=field.at[s, :, pl.ds(1, 2 * NB), pl.ds(there, 1), :],
                send_sem=hs_sem.at[side, s],
                recv_sem=hr_sem.at[side, s, 0],
                device_id=(sub, to),
                device_id_type=MESH,
            ).wait_send()


def per_device(
    load_current, diagonal, start_field, block_inverse, multipliers, active_rows,
    contact_peer, contact_len, port_row, port_col, port_current,
):
    width = load_current.shape[3]

    def tiled(x):
        return x.reshape(2, 8, 8, width // 128, 128).transpose(0, 1, 3, 2, 4)

    def stay(x):
        return pltpu.with_memory_space_constraint(x, pltpu.HBM)

    blocks = (
        block_inverse.reshape(NB, 2, 256, 2, 2, 128).transpose(0, 1, 2, 4, 3, 5).reshape(NB, 2048, 128)
    )
    hbm = pl.BlockSpec(memory_space=pltpu.HBM)
    vmem = pl.BlockSpec(memory_space=pltpu.VMEM)
    dma = pltpu.SemaphoreType.DMA
    solved, following = pl.pallas_call(
        body,
        out_shape=(
            jax.ShapeDtypeStruct((2, 8, 2 * NB, 8, 128), F32),
            jax.ShapeDtypeStruct(multipliers.shape, F32),
        ),
        in_specs=[hbm] * 12,
        out_specs=(vmem, vmem),
        scratch_shapes=[
            pltpu.VMEM((4, 2, 2 * NB + 2, ROWS + 16, 128), F32),
            pltpu.VMEM((2, 8, 2 * NB, 8, 128), F32),
            pltpu.VMEM((2, 8, 2 * NB, 8, 128), F32),
            pltpu.VMEM((NB, 2048, 128), F32),
            pltpu.VMEM((NB // 2, 512, 512), BF),
            pltpu.VMEM((NB // 2, 512, 512), BF),
            pltpu.VMEM((NB // 2, 512, 512), BF),
            pltpu.VMEM((NB // 2, 512, 512), BF),
            pltpu.VMEM((2 * ROWS, 512), BF),
            pltpu.VMEM((2 * ROWS, 512), BF),
            pltpu.VMEM((8, 2, ROWS, 128), F32),
            pltpu.VMEM((8, 2, ROWS, 128), F32),
            pltpu.VMEM((2, ROWS, 128), F32),
            pltpu.VMEM((2, 2, ROWS, 128), F32),
            pltpu.VMEM((2, ROWS, 128), F32),
            pltpu.VMEM((2, ROWS, 128), F32),
            pltpu.VMEM((ROWS, 16), F32),
            pltpu.VMEM((8, 16), jnp.int32),
            pltpu.VMEM((8, 16), jnp.int32),
            pltpu.VMEM((1, 16), jnp.int32),
            pltpu.VMEM((1, 16), jnp.int32),
            pltpu.VMEM((2, 16), F32),
            pltpu.VMEM((4 * ROWS, 16), BF),
            pltpu.SMEM((16,), jnp.int32),
            dma((NB, 6)),
            dma((NB,)),
            dma((7,)),
            dma((2, 3)),
            dma((2, 3, NB // 2)),
            dma((7,)),
            dma((8,)),
            dma((7,)),
            dma((8,)),
            dma((4,)),
        ],
        compiler_params=pltpu.CompilerParams(
            collective_id=0, has_side_effects=True, vmem_limit_bytes=51 * 2**20
        ),
        name="relax",
    )(
        tiled(load_current), tiled(diagonal), start_field, tiled(start_field), blocks, stay(multipliers),
        stay(active_rows), stay(contact_len.T), stay(contact_peer.T), stay(port_row), stay(port_col),
        stay(port_current[0]),
    )
    return solved.transpose(0, 1, 3, 2, 4).reshape(load_current.shape), following


def solution(mesh):
    check_order()
    in_specs = (
        P("sub", None, "tile", None),
        P("sub", None, "tile", None),
        P("sub", None, "tile", None),
        P("sub", None, None, None, None, None),
        P("sub", None, "tile", None),
        P(),
        P(),
        P(),
        P("sub", None),
        P("sub", None),
        P("sub", None, None),
    )
    out_specs = (P("sub", None, "tile", None), P("sub", None, "tile", None))
    return jax.shard_map(
        per_device, mesh=mesh, in_specs=in_specs, out_specs=out_specs, check_vma=False
    )
```
